128 devices in a mesh: gx: 8 (over x_lo, z), gy: 16 (over x_hi, y, core).
Axes of the slice: x: 4 (x_hi: 2, x_lo: 2; x = x_hi * 2 + x_lo), y: 4, z: 4, core: 2. Of those that a mesh axis runs over, the one named last changes fastest.
Arguments:
- scalars: float32 [4, 64, 128, 2048], P(None, None, 'gx', 'gy'), may hold values from -6 to 6
- winds: float32 [2, 64, 128, 2048], P(None, None, 'gx', 'gy'), may hold values from -0.6 to 0.6
- map_factor: float32 [128, 2048], P('gx', 'gy'), may hold values from 0.7 to 1.3
- urban_counts: int32 [128], P(('gx', 'gy')), may hold values from 256 to 1024, as said below
- urban_cols: int32 [131072], P(('gx', 'gy')), may hold values from 0 to 2047, as said below
- street_class: int32 [131072], P(('gx', 'gy')), may hold values from 0 to 9
- area_table: float32 [10, 10], replicated, may hold values from 0.2 to 1
- wall_temp: float32 [10, 131072], P(None, ('gx', 'gy')), may hold values from -6 to 6
- indoor_temp: float32 [131072], P(('gx', 'gy')), may hold values from -6 to 6
Outputs:
- scalars_out: float32 [4, 64, 128, 2048], P(None, None, 'gx', 'gy')
- wall_out: float32 [10, 131072], P(None, ('gx', 'gy'))
- indoor_out: float32 [131072], P(('gx', 'gy'))
The draws below stay inside these ranges and needn't reach their ends.
Inputs may be any that keep to these rules, and one draw needn't show every extreme that they name: `urban_counts`: some tile has exactly 1024 live urban columns. `urban_cols`: the 1024 entries of each tile are distinct cells of that tile, numbered x * 128 + y within it.
All inputs are finite; a program needn't handle non-finite values.
Results may differ from the reference program's by a relative error of at most 0.000056.
Values sent between devices are 32-bit elements; how exact they have to be, the bound alone decides.
A program may use at most 192 MiB of HBM per device.

```python
import jax
import jax.numpy as jnp
from jax import lax

CX = 16
CY = 128
LEV = 64
NSC = 4
UL = 10
NWL = 10
NCLS = 10
CAP = 1024
NX = 128
NY = 2048
N_GY = 16
DEVICES = 128


def draw_urban_counts(key, part):
    counts = jax.random.randint(key, (DEVICES,), CAP // 4, CAP + 1)
    chosen = jax.random.randint(jax.random.fold_in(key, 7), (), 0, DEVICES)
    return counts.at[chosen].set(CAP).astype(jnp.int32)


def draw_urban_cols(key, part):
    keys = jax.random.split(key, DEVICES)

    def one_tile(tile_key):
        return jax.random.permutation(tile_key, CX * CY)[:CAP]
    return jax.vmap(one_tile)(keys).reshape(-1).astype(jnp.int32)


def plant(values, own_key, least, top_value):
    shape = values.shape
    spot = [jax.random.randint(jax.random.fold_in(own_key, axis), (), 0, shape[axis]) for axis in range(len(shape))]
    values = values.at[tuple(spot)].set(least)
    longest = shape.index(max(shape))
    spot[longest] = (spot[longest] + 1) % shape[longest]
    return values.at[tuple(spot)].set(top_value)


def block_scale(stream_key, shape, cuts, smallest, high):
    factor_of, own = 1.0, jax.random.fold_in(stream_key, 6)
    for axis_at, parts in cuts:
        draws = jnp.exp(jax.random.uniform(jax.random.fold_in(own, axis_at), (parts,), jnp.float32, smallest / len(cuts), high / len(cuts)))
        factor_of = factor_of * jnp.repeat(draws, shape[axis_at] // parts).reshape([-1 if axis == axis_at else 1 for axis in range(len(shape))])
    return factor_of


def gaussian(key, dims, spread, bound, shards=(), kind=jnp.bfloat16):
    drawn = jax.random.normal(key, dims, jnp.float32) * spread
    if len(shards) > 0:
        drawn = block_scale(key, dims, shards, -0.22, 0.18) * drawn
    return jnp.clip(drawn, min=-bound, max=bound).astype(kind)


def setup_inputs(seed: int = 0) -> dict:
    key_of = jax.random.split(jax.random.key(seed), 10)
    scalars = gaussian(key_of[0], (NSC, LEV, NX, NY), 1.0, 6.0, ((2, 8), (3, 16)), jnp.float32)
    winds = jnp.clip(jax.random.uniform(key_of[1], (2, LEV, NX, NY), jnp.float32, -0.6, 0.6) * block_scale(key_of[1], (2, LEV, NX, NY), ((2, 8), (3, 16)), -0.4, 0.0), -0.6, 0.6)
    map_factor = jnp.clip(1.0 + 0.06 * jax.random.normal(key_of[2], (NX, NY), jnp.float32), 0.7, 1.3)
    urban_counts = draw_urban_counts(jax.random.fold_in(key_of[9], 71), 0)
    urban_cols = draw_urban_cols(jax.random.fold_in(key_of[9], 71), 0)
    street_class = plant(jax.random.randint(key_of[5], (DEVICES * CAP,), 0, NCLS), jax.random.fold_in(key_of[5], 1), 0, NCLS - 1).astype(jnp.int32)
    area_table = jnp.clip(jax.random.uniform(key_of[6], (NCLS, UL), jnp.float32, 0.2, 1.0), 0.2, 1.0)
    wall_temp = gaussian(key_of[7], (NWL, DEVICES * CAP), 1.0, 6.0, ((1, 128),), jnp.float32)
    indoor_temp = gaussian(key_of[8], (DEVICES * CAP,), 1.0, 6.0, ((0, 128),), jnp.float32)
    return dict(scalars=scalars, winds=winds, map_factor=map_factor, urban_counts=urban_counts, urban_cols=urban_cols, street_class=street_class, area_table=area_table, wall_temp=wall_temp, indoor_temp=indoor_temp)


heat_coef = 0.5
wall_coef = 0.05
conduct = 0.3
inner_coef = 0.2
room_coef = 0.1
flux_coef = 0.5


def face_divergence(field, speed, axis):
    shifted = [jnp.roll(field, -(offset - 2), axis) for offset in range(6)]
    face_speed = 0.5 * (speed + jnp.roll(speed, -1, axis))
    flux = face_speed * (37.0 * (shifted[2] + shifted[3]) - 8.0 * (shifted[1] + shifted[4]) + (shifted[0] + shifted[5])) / 60.0
    flux = flux - jnp.abs(face_speed) * ((shifted[5] - shifted[0]) - 5.0 * (shifted[4] - shifted[1]) + 10.0 * (shifted[3] - shifted[2])) / 60.0
    return flux - jnp.roll(flux, 1, axis)


def physics(packed):
    air_temp = packed[:UL]
    areas = packed[UL:2 * UL]
    walls = packed[2 * UL:2 * UL + NWL]
    indoor = packed[2 * UL + NWL]
    heat = heat_coef * areas * (walls[0] - air_temp)
    first = walls[0] - wall_coef * jnp.sum(heat, axis=0) + conduct * (walls[1] - walls[0])
    middle = walls[1:-1] + conduct * (walls[:-2] - 2.0 * walls[1:-1] + walls[2:])
    last = walls[-1] + conduct * (walls[-2] - walls[-1]) + inner_coef * (indoor - walls[-1])
    indoor_new = indoor + room_coef * (walls[-1] - indoor)
    return jnp.concatenate([heat, first[None], middle, last[None], indoor_new[None]], axis=0)


def reference(scalars, winds, map_factor, urban_counts, urban_cols, street_class, area_table, wall_temp, indoor_temp):
    square = map_factor * map_factor

    def tendency(field):
        return -square * (face_divergence(field, winds[0], 1) + face_divergence(field, winds[1], 2))

    def advance(field):
        section_one = field + tendency(field) / 3.0
        section_two = field + tendency(section_one) / 2.0
        return field + tendency(section_two)

    advanced = lax.map(advance, scalars)
    device = jnp.arange(DEVICES, dtype=jnp.int32)
    row_tile = (device // N_GY)[:, None]
    col_tile = (device % N_GY)[:, None]
    cells = urban_cols.reshape(DEVICES, CAP)
    west = row_tile * CX + cells // CY
    south = col_tile * CY + cells % CY
    flat = (west * NY + south).reshape(-1).astype(jnp.int32)
    lower = advanced[0, :UL].reshape(UL, NX * NY)
    air_temp = lower[:, flat]
    areas = area_table.T[:, street_class]
    packed = jnp.concatenate([air_temp, areas, wall_temp, indoor_temp[None]], axis=0)
    result = physics(packed)
    live = (jnp.arange(CAP, dtype=jnp.int32)[None, :] < urban_counts[:, None]).reshape(-1)
    heating = jnp.where(live[None, :], flux_coef * result[:UL], 0.0)
    lower = lower.at[:, flat].add(heating).reshape(UL, NX, NY)
    scalars_out = advanced.at[0, :UL].set(lower)
    wall_out = jnp.where(live[None, :], result[UL:UL + NWL], wall_temp)
    indoor_out = jnp.where(live, result[UL + NWL], indoor_temp)
    return (scalars_out, wall_out, indoor_out)
```

```python
import jax
import jax.numpy as jnp
from jax import lax
from jax.experimental import pallas as pl
from jax.experimental.pallas import tpu as pltpu
from jax.sharding import PartitionSpec as P

MESH = pl.DeviceIdType.MESH
UL = 10
NWL = 10
LOW = 16

heat_coef = 0.5
wall_coef = 0.05
conduct = 0.3
inner_coef = 0.2
room_coef = 0.1
flux_coef = 0.5

CX = 16
LANES = 128
NSC = 4
LEV = 64
ROWS = 8
CHUNKS = LEV // ROWS
H = 3
EDGE_X = (0, 1, 2, 13, 14, 15)
INNER_X = tuple(range(3, 13))


def roll(value, shift):
    return pltpu.roll(value, shift % LANES, 1)


def flux_terms(m3, m2, m1, q, p1, p2, speed):
    even = 37.0 * (m1 + q) - 8.0 * (m2 + p1) + (m3 + p2)
    odd = (p2 - m3) - 5.0 * (p1 - m2) + 10.0 * (q - m1)
    return speed * even - jnp.abs(speed) * odd


def step_kernel(
    scal, wind, mapf, out,
    field, windx, windy, facex, facey, facee, square, own, give_n, give_s, got_s, got_n, result, wpack, wgot, mapbuf,
    load_s, load_w, load_m, sx, rx, sy, ry, swx, rwx, swy, rwy, store_o,
):
    gx, gy = lax.axis_index("gx"), lax.axis_index("gy")
    nx, ny = lax.axis_size("gx"), lax.axis_size("gy")
    east, west = {"gx": lax.rem(gx + 1, nx)}, {"gx": lax.rem(gx + nx - 1, nx)}
    north, south = {"gy": lax.rem(gy + 1, ny)}, {"gy": lax.rem(gy + ny - 1, ny)}

    barrier = pltpu.get_barrier_semaphore()
    for device in (east, west, north, south):
        pl.semaphore_signal(barrier, inc=1, device_id=device, device_id_type=MESH)

    def load_scalar(s, x):
        return pltpu.make_async_copy(scal.at[s, :, x, :], field.at[0, H + x, s], load_s.at[s, x])

    def load_wind(which, x):
        target = windx.at[1 + x] if which == 0 else windy.at[x]
        return pltpu.make_async_copy(wind.at[which, :, x, :], target, load_w.at[which, x])

    load_map = pltpu.make_async_copy(mapf, mapbuf, load_m)
    for s in range(NSC):
        for x in EDGE_X:
            load_scalar(s, x).start()
    load_wind(0, 0).start()
    load_wind(0, CX - 1).start()
    for x in range(CX):
        load_wind(1, x).start()
    for s in range(NSC):
        for x in INNER_X:
            load_scalar(s, x).start()
    for x in range(1, CX - 1):
        load_wind(0, x).start()
    load_map.start()

    def remote(src, dst, send, recv, device):
        return pltpu.make_async_remote_copy(
            src_ref=src, dst_ref=dst, send_sem=send, recv_sem=recv, device_id=device, device_id_type=MESH
        )

    def rows_of(k):
        return pl.ds(pl.multiple_of(k * ROWS, ROWS), ROWS)

    def x_copies(sec, k):
        rows = rows_of(k)
        return (
            remote(field.at[sec, pl.ds(CX, H), :, rows, :], field.at[sec, pl.ds(0, H), :, rows, :],
                   sx.at[sec, k, 0], rx.at[sec, k, 0], east),
            remote(field.at[sec, pl.ds(H, H), :, rows, :], field.at[sec, pl.ds(CX + H, H), :, rows, :],
                   sx.at[sec, k, 1], rx.at[sec, k, 1], west),
        )

    def y_copies(sec, k):
        return (
            remote(give_n.at[sec, k], got_s.at[sec, k], sy.at[sec, k, 0], ry.at[sec, k, 0], north),
            remote(give_s.at[sec, k], got_n.at[sec, k], sy.at[sec, k, 1], ry.at[sec, k, 1], south),
        )

    wx_copies = (
        remote(windx.at[CX], windx.at[0], swx.at[0], rwx.at[0], east),
        remote(windx.at[1], windx.at[CX + 1], swx.at[1], rwx.at[1], west),
    )
    wy_copies = (
        remote(wpack.at[0], wgot.at[0], swy.at[0], rwy.at[0], north),
        remote(wpack.at[1], wgot.at[1], swy.at[1], rwy.at[1], south),
    )

    for s in range(NSC):
        for x in EDGE_X:
            load_scalar(s, x).wait()
    load_wind(0, 0).wait()
    load_wind(0, CX - 1).wait()
    pl.semaphore_wait(barrier, 4)
    for copy in wx_copies:
        copy.start()

    def send_first(k, carry):
        for copy in x_copies(0, k):
            copy.start()
        return carry

    lax.fori_loop(0, CHUNKS, send_first, 0)

    lane = lax.broadcasted_iota(jnp.int32, (ROWS, LANES), 1)
    slot = lane // 8
    inside = lane % 8
    low = inside < 3

    def pack_send(sec, k, pair, first, second):
        give_n[sec, k, pair] = jnp.where(low, first, roll(second, 3))
        give_s[sec, k, pair] = jnp.where(low, roll(first, -3), second)

    for x in range(CX):
        load_wind(1, x).wait()
    to_n = jnp.zeros((ROWS, LANES), jnp.float32)
    to_s = jnp.zeros((ROWS, LANES), jnp.float32)
    for k in range(CHUNKS):
        packed = jnp.zeros((ROWS, LANES), jnp.float32)
        for x in range(CX):
            packed = jnp.where(slot == x, roll(windy[x, pl.ds(k * ROWS, ROWS), :], 8 * x + 3), packed)
        to_n = jnp.where(inside == k, roll(packed, k - 2), to_n)
        to_s = jnp.where(inside == k, roll(packed, k - 3), to_s)
        facee[pl.ds(k * ROWS, ROWS), :] = packed
    wpack[0] = to_n
    wpack[1] = to_s
    for copy in wy_copies:
        copy.start()

    for s in range(NSC):
        for x in INNER_X:
            load_scalar(s, x).wait()

    def pack_first(k, carry):
        rows = rows_of(k)
        for pair in range(2):
            packs = []
            for s in (2 * pair, 2 * pair + 1):
                packed = jnp.zeros((ROWS, LANES), jnp.float32)
                for x in range(CX):
                    packed = jnp.where(slot == x, roll(field[0, H + x, s, rows, :], 8 * x + 3), packed)
                own[0, s, rows, :] = packed
                packs.append(packed)
            pack_send(0, k, pair, *packs)
        for copy in y_copies(0, k):
            copy.start()
        return carry

    lax.fori_loop(0, CHUNKS, pack_first, 0)

    load_map.wait()
    for x in range(CX):
        factor = jnp.broadcast_to(mapbuf[pl.ds(x, 1), :], (ROWS, LANES))
        minus = factor * factor
        square[0, x] = minus * (1.0 / 3.0)
        square[1, x] = minus * 0.5
        square[2, x] = minus
    for x in range(1, CX - 1):
        load_wind(0, x).wait()
    for copy in wx_copies:
        copy.wait_recv()
    for copy in wy_copies:
        copy.wait_recv()

    from_s = wgot[0]
    from_n = wgot[1]
    for k in range(CHUNKS):
        rows = pl.ds(k * ROWS, ROWS)
        for x in range(CX + 1):
            facex[x, rows, :] = (windx[x, rows, :] + windx[x + 1, rows, :]) * (1.0 / 120.0)
        behind = roll(from_s, 2 - k)
        ahead = roll(from_n, 3 - k)
        packed = jnp.where(low, facee[rows, :], ahead)
        facee[rows, :] = (roll(packed, 1) + packed) * (1.0 / 120.0)
        for x in range(CX):
            centre = windy[x, rows, :]
            halo = roll(behind, -(8 * x + 3))
            facey[x, rows, :] = (roll(jnp.where(lane == 127, halo, centre), 1) + centre) * (1.0 / 120.0)

    def section(sec, k, last):
        rows = rows_of(k)
        for pair in range(2):
            packs = []
            from_south, from_north = got_s[sec, k, pair], got_n[sec, k, pair]
            for part in range(2):
                s = 2 * pair + part
                mine = own[sec, s, rows, :]
                if part == 0:
                    before, after = from_south, roll(from_north, 3)
                else:
                    before, after = roll(from_south, -3), from_north
                merged = jnp.where(low, before, after)
                edge = jnp.where(low, mine, after)
                end = flux_terms(
                    roll(edge, 3), roll(edge, 2), roll(edge, 1), edge, roll(edge, -1), roll(edge, -2), facee[rows, :]
                )
                q = [field[sec, i, s, rows, :] for i in range(CX + 2 * H)]
                g = [q[i + 1] - q[i] for i in range(CX + 2 * H - 1)]
                d2 = {i: g[i] - g[i - 1] for i in range(1, CX + 2 * H - 1)}
                d3 = {i: d2[i + 1] - d2[i] for i in range(1, CX + 2 * H - 2)}
                d4 = {i: d3[i] - d3[i - 1] for i in range(2, CX + 2 * H - 2)}
                even = {i: (d4[i] - 5.0 * d2[i]) + 30.0 * q[i] for i in range(2, CX + 2 * H - 2)}
                flux = []
                for f in range(CX + 1):
                    speed = facex[f, rows, :]
                    flux.append(speed * (even[f + 2] + even[f + 3]) - jnp.abs(speed) * (d4[f + 3] - d4[f + 2]))
                packed = jnp.zeros((ROWS, LANES), jnp.float32)
                for x in range(CX):
                    c = q[H + x]
                    halo = roll(merged, -(8 * x + 3))
                    m1 = roll(jnp.where(lane >= 127, halo, c), 1)
                    m2 = roll(jnp.where(lane >= 126, halo, c), 2)
                    m3 = roll(jnp.where(lane >= 125, halo, c), 3)
                    p1 = roll(jnp.where(lane < 1, halo, c), -1)
                    p2 = roll(jnp.where(lane < 2, halo, c), -2)
                    across = flux_terms(m3, m2, m1, c, p1, p2, facey[x, rows, :])
                    ending = roll(end, -(8 * x + 3))
                    total = (flux[x + 1] - flux[x]) + (roll(jnp.where(lane == 0, ending, across), -1) - across)
                    base = field[0, H + x, s, rows, :]
                    new = base - square[sec, x] * total
                    if last:
                        result[x, s, rows, :] = new
                    else:
                        field[sec + 1, H + x, s, rows, :] = new
                        packed = jnp.where(slot == x, roll(new, 8 * x + 3), packed)
                if not last:
                    own[sec + 1, s, rows, :] = packed
                    packs.append(packed)
            if not last:
                pack_send(sec + 1, k, pair, *packs)

    def early(step, carry):
        sec, k = step // CHUNKS, lax.rem(step, CHUNKS)
        for copy in x_copies(sec, k) + y_copies(sec, k):
            copy.wait_recv()
        section(sec, k, False)
        for copy in x_copies(sec + 1, k) + y_copies(sec + 1, k):
            copy.start()
        return carry

    lax.fori_loop(0, 2 * CHUNKS, early, 0)

    def store(k):
        rows = rows_of(k)
        return pltpu.make_async_copy(result.at[:, :, rows, :], out.at[:, :, rows, :], store_o.at[k])

    def late(k, carry):
        for copy in x_copies(2, k) + y_copies(2, k):
            copy.wait_recv()
        section(2, k, True)
        store(k).start()
        return carry

    lax.fori_loop(0, CHUNKS, late, 0)

    for copy in wx_copies + wy_copies:
        copy.wait_send()

    def finish(step, carry):
        sec, k = step // CHUNKS, lax.rem(step, CHUNKS)
        for copy in x_copies(sec, k) + y_copies(sec, k):
            copy.wait_send()
        return carry

    lax.fori_loop(0, 3 * CHUNKS, finish, 0)

    def stored(k, carry):
        store(k).wait()
        return carry

    lax.fori_loop(0, CHUNKS, stored, 0)


def advance(scalars, winds, map_factor):
    f32 = jnp.float32
    dma = pltpu.SemaphoreType.DMA
    return pl.pallas_call(
        step_kernel,
        out_shape=jax.ShapeDtypeStruct((CX, NSC, LEV, LANES), f32),
        in_specs=[pl.BlockSpec(memory_space=pl.ANY)] * 3,
        out_specs=pl.BlockSpec(memory_space=pl.ANY),
        scratch_shapes=[
            pltpu.VMEM((3, CX + 2 * H, NSC, LEV, LANES), f32),
            pltpu.VMEM((CX + 2, LEV, LANES), f32),
            pltpu.VMEM((CX, LEV, LANES), f32),
            pltpu.VMEM((CX + 1, LEV, LANES), f32),
            pltpu.VMEM((CX, LEV, LANES), f32),
            pltpu.VMEM((LEV, LANES), f32),
            pltpu.VMEM((3, CX, ROWS, LANES), f32),
            pltpu.VMEM((3, NSC, LEV, LANES), f32),
            pltpu.VMEM((3, CHUNKS, 2, ROWS, LANES), f32),
            pltpu.VMEM((3, CHUNKS, 2, ROWS, LANES), f32),
            pltpu.VMEM((3, CHUNKS, 2, ROWS, LANES), f32),
            pltpu.VMEM((3, CHUNKS, 2, ROWS, LANES), f32),
            pltpu.VMEM((CX, NSC, LEV, LANES), f32),
            pltpu.VMEM((2, ROWS, LANES), f32),
            pltpu.VMEM((2, ROWS, LANES), f32),
            pltpu.VMEM((CX, LANES), f32),
            dma((NSC, CX)),
            dma((2, CX)),
            dma(()),
            dma((3, CHUNKS, 2)),
            dma((3, CHUNKS, 2)),
            dma((3, CHUNKS, 2)),
            dma((3, CHUNKS, 2)),
            dma((2,)),
            dma((2,)),
            dma((2,)),
            dma((2,)),
            dma((CHUNKS,)),
        ],
        compiler_params=pltpu.CompilerParams(collective_id=0, has_side_effects=True, vmem_limit_bytes=24 << 20),
        name="advance",
    )(scalars, winds, map_factor)


def urban_kernel(
    adv, counts, cols, classes, table, wall, indoor, out, wall_out, indoor_out, body, low_in, low_out, heat_pad, sem_in, sem_low, sem_out
):
    load_low = pltpu.make_async_copy(adv.at[:, 0, pl.ds(0, LOW), :], low_in, sem_in)
    load_low.start()
    rest = []
    for x in range(CX):
        rest.append(pltpu.make_async_copy(adv.at[x, 0, pl.ds(LOW, LEV - LOW), :], out.at[0, pl.ds(LOW, LEV - LOW), x, :], sem_out.at[0, x]))
        for s in range(1, NSC):
            rest.append(pltpu.make_async_copy(adv.at[x, s], out.at[s, :, x, :], sem_out.at[s, x]))
    for copy in rest:
        copy.start()
    slots = cols.shape[1]
    column = cols[...]
    col_x = column // LANES
    col_y = column % LANES
    live = lax.broadcasted_iota(jnp.int32, (1, slots), 1) < counts[0]
    onehot = (lax.broadcasted_iota(jnp.int32, (LANES, slots), 0) == col_y).astype(jnp.float32)
    ncls = table.shape[0]
    picked = (lax.broadcasted_iota(jnp.int32, (ncls, slots), 0) == classes[...]).astype(jnp.float32)
    areas = lax.dot_general(
        table[...], picked, (((0,), (0,)), ((), ())), precision=lax.Precision.HIGHEST, preferred_element_type=jnp.float32
    )
    load_low.wait()
    gathered = jnp.dot(
        low_in[...].reshape(CX * LOW, LANES), onehot, precision=lax.Precision.HIGHEST, preferred_element_type=jnp.float32
    ).reshape(CX, LOW, slots)
    air = jnp.zeros((LOW, slots), jnp.float32)
    for x in range(CX):
        air = jnp.where(col_x == x, gathered[x], air)
    walls = wall[...]
    room = indoor[...]
    top = walls[0:1]
    heat = heat_coef * areas * (top - air[:UL])
    first = top - wall_coef * jnp.sum(heat, axis=0, keepdims=True) + conduct * (walls[1:2] - top)
    middle = walls[1:-1] + conduct * (walls[:-2] - 2.0 * walls[1:-1] + walls[2:])
    bottom = walls[NWL - 1 : NWL]
    last = bottom + conduct * (walls[NWL - 2 : NWL - 1] - bottom) + inner_coef * (room - bottom)
    wall_out[0:1] = jnp.where(live, first, top)
    wall_out[1 : NWL - 1] = jnp.where(live, middle, walls[1:-1])
    wall_out[NWL - 1 : NWL] = jnp.where(live, last, bottom)
    indoor_out[...] = jnp.where(live, room + room_coef * (bottom - room), room)
    heat_pad[...] = jnp.zeros_like(heat_pad)
    heat_pad[0:UL] = jnp.where(live, flux_coef * heat, 0.0)
    padded = heat_pad[...]
    for x in range(CX):
        body[x] = jnp.where(col_x == x, padded, 0.0)
    spread = lax.dot_general(
        body[...].reshape(CX * LOW, slots), onehot, (((1,), (1,)), ((), ())),
        precision=lax.Precision.HIGHEST, preferred_element_type=jnp.float32,
    )
    low_out[...] = low_in[...] + spread.reshape(CX, LOW, LANES)
    final = [pltpu.make_async_copy(low_out.at[x], out.at[0, pl.ds(0, LOW), x, :], sem_low.at[x]) for x in range(CX)]
    for copy in final:
        copy.start()
    for copy in rest + final:
        copy.wait()


def urban(adv, counts, cols, classes, table, wall, indoor):
    f32 = jnp.float32
    slots = wall.shape[1]
    vmem = pl.BlockSpec(memory_space=pltpu.VMEM)
    anywhere = pl.BlockSpec(memory_space=pl.ANY)
    dma = pltpu.SemaphoreType.DMA
    return pl.pallas_call(
        urban_kernel,
        out_shape=(
            jax.ShapeDtypeStruct((NSC, LEV, CX, LANES), f32),
            jax.ShapeDtypeStruct((NWL, slots), f32),
            jax.ShapeDtypeStruct((1, slots), f32),
        ),
        in_specs=[anywhere, pl.BlockSpec(memory_space=pltpu.SMEM)] + [vmem] * 5,
        out_specs=(anywhere, vmem, vmem),
        scratch_shapes=[
            pltpu.VMEM((CX, LOW, slots), f32),
            pltpu.VMEM((CX, LOW, LANES), f32),
            pltpu.VMEM((CX, LOW, LANES), f32),
            pltpu.VMEM((LOW, slots), f32),
            dma(()),
            dma((CX,)),
            dma((NSC, CX)),
        ],
        compiler_params=pltpu.CompilerParams(vmem_limit_bytes=16 << 20),
        name="urban",
    )(adv, counts, cols.reshape(1, slots), classes.reshape(1, slots), table, wall, indoor.reshape(1, slots))


def per_device(scalars, winds, map_factor, urban_counts, urban_cols, street_class, area_table, wall_temp, indoor_temp):
    adv = advance(scalars, winds, map_factor)
    scalars_out, wall_out, indoor_out = urban(
        adv, urban_counts, urban_cols, street_class, area_table, wall_temp, indoor_temp
    )
    return (scalars_out, wall_out, indoor_out.reshape(indoor_temp.shape))


def solution(mesh):
    in_specs = (
        P(None, None, "gx", "gy"),
        P(None, None, "gx", "gy"),
        P("gx", "gy"),
        P(("gx", "gy")),
        P(("gx", "gy")),
        P(("gx", "gy")),
        P(),
        P(None, ("gx", "gy")),
        P(("gx", "gy")),
    )
    out_specs = (P(None, None, "gx", "gy"), P(None, ("gx", "gy")), P(("gx", "gy")))
    return jax.shard_map(per_device, mesh=mesh, in_specs=in_specs, out_specs=out_specs, check_vma=False)
```

```python
import jax
import jax.numpy as jnp
from jax import lax
from jax.experimental import pallas as pl
from jax.experimental.pallas import tpu as pltpu
from jax.sharding import PartitionSpec as P

MESH = pl.DeviceIdType.MESH
UL = 10
NWL = 10
LOW = 16

heat_coef = 0.5
wall_coef = 0.05
conduct = 0.3
inner_coef = 0.2
room_coef = 0.1
flux_coef = 0.5

CX = 16
LANES = 128
NSC = 4
LEV = 64
ROWS = 8
CHUNKS = LEV // ROWS
H = 3
EDGE_X = (0, 1, 2, 13, 14, 15)
INNER_X = tuple(range(3, 13))


def roll(value, shift):
    return pltpu.roll(value, shift % LANES, 1)


def split(value):
    high = value.astype(jnp.bfloat16)
    return high, (value - high.astype(jnp.float32)).astype(jnp.bfloat16)


def fill_stencil(stencil):
    row = lax.broadcasted_iota(jnp.int32, (LANES, LANES), 0)
    column = lax.broadcasted_iota(jnp.int32, (LANES, LANES), 1)
    halo = jnp.where(row >= LANES - H, row - LANES, jnp.where(row < H, row + LANES, 4 * LANES))
    for source, cell in enumerate((row, halo)):
        for block in range(4):
            offset = cell - column + (2 if block < 2 else 3)
            weights = (1.0, -8.0, 37.0, 37.0, -8.0, 1.0) if block % 2 == 0 else (-1.0, 5.0, -10.0, 10.0, -5.0, 1.0)
            band = jnp.zeros((LANES, LANES), jnp.float32)
            for at, weight in enumerate(weights):
                band = jnp.where(offset == at, weight, band)
            band = band.astype(jnp.bfloat16)
            for part in range(2):
                stencil[pl.ds((2 * source + part) * LANES, LANES), pl.ds(block * LANES, LANES)] = band


def step_kernel(
    scal, wind, mapf, out,
    field, windx, windy, facex, facex_abs, face_r, face_r_abs, face_l, face_l_abs, square, give_n, give_s, got_s, got_n,
    result, wpack, wgot, mapbuf, stencil, cells, across,
    load_s, load_w, load_m, sx, rx, sy, ry, swx, rwx, swy, rwy, store_o,
):
    gx, gy = lax.axis_index("gx"), lax.axis_index("gy")
    nx, ny = lax.axis_size("gx"), lax.axis_size("gy")
    east, west = {"gx": lax.rem(gx + 1, nx)}, {"gx": lax.rem(gx + nx - 1, nx)}
    north, south = {"gy": lax.rem(gy + 1, ny)}, {"gy": lax.rem(gy + ny - 1, ny)}

    barrier = pltpu.get_barrier_semaphore()
    for device in (east, west, north, south):
        pl.semaphore_signal(barrier, inc=1, device_id=device, device_id_type=MESH)

    def load_scalar(s, x):
        return pltpu.make_async_copy(scal.at[s, :, x, :], field.at[0, H + x, s], load_s.at[s, x])

    def load_wind(which, x):
        target = windx.at[1 + x] if which == 0 else windy.at[x]
        return pltpu.make_async_copy(wind.at[which, :, x, :], target, load_w.at[which, x])

    load_map = pltpu.make_async_copy(mapf, mapbuf, load_m)
    for s in range(NSC):
        for x in EDGE_X:
            load_scalar(s, x).start()
    load_wind(0, 0).start()
    load_wind(0, CX - 1).start()
    for x in range(CX):
        load_wind(1, x).start()
    for s in range(NSC):
        for x in INNER_X:
            load_scalar(s, x).start()
    for x in range(1, CX - 1):
        load_wind(0, x).start()
    load_map.start()

    def remote(src, dst, send, recv, device):
        return pltpu.make_async_remote_copy(
            src_ref=src, dst_ref=dst, send_sem=send, recv_sem=recv, device_id=device, device_id_type=MESH
        )

    def rows_of(k):
        return pl.ds(pl.multiple_of(k * ROWS, ROWS), ROWS)

    def x_copies(sec, k):
        rows = rows_of(k)
        return (
            remote(field.at[sec, pl.ds(CX, H), :, rows, :], field.at[sec, pl.ds(0, H), :, rows, :],
                   sx.at[sec, k, 0], rx.at[sec, k, 0], east),
            remote(field.at[sec, pl.ds(H, H), :, rows, :], field.at[sec, pl.ds(CX + H, H), :, rows, :],
                   sx.at[sec, k, 1], rx.at[sec, k, 1], west),
        )

    def y_copies(sec, k):
        return (
            remote(give_n.at[sec, k], got_s.at[sec, k], sy.at[sec, k, 0], ry.at[sec, k, 0], north),
            remote(give_s.at[sec, k], got_n.at[sec, k], sy.at[sec, k, 1], ry.at[sec, k, 1], south),
        )

    wx_copies = (
        remote(windx.at[CX], windx.at[0], swx.at[0], rwx.at[0], east),
        remote(windx.at[1], windx.at[CX + 1], swx.at[1], rwx.at[1], west),
    )
    wy_copies = (
        remote(wpack.at[0], wgot.at[0], swy.at[0], rwy.at[0], north),
        remote(wpack.at[1], wgot.at[1], swy.at[1], rwy.at[1], south),
    )

    fill_stencil(stencil)
    for s in range(NSC):
        for x in EDGE_X:
            load_scalar(s, x).wait()
    load_wind(0, 0).wait()
    load_wind(0, CX - 1).wait()
    pl.semaphore_wait(barrier, 4)
    for copy in wx_copies:
        copy.start()

    def send_first(k, carry):
        for copy in x_copies(0, k):
            copy.start()
        return carry

    lax.fori_loop(0, CHUNKS, send_first, 0)

    lane = lax.broadcasted_iota(jnp.int32, (ROWS, LANES), 1)
    slot = lane // 8
    inside = lane % 8
    low = inside < 3

    def pack_send(sec, k, pair, first, second):
        give_n[sec, k, pair] = jnp.where(low, first, roll(second, 3))
        give_s[sec, k, pair] = jnp.where(low, roll(first, -3), second)

    for x in range(CX):
        load_wind(1, x).wait()
    to_n = jnp.zeros((ROWS, LANES), jnp.float32)
    to_s = jnp.zeros((ROWS, LANES), jnp.float32)
    for k in range(CHUNKS):
        packed = jnp.zeros((ROWS, LANES), jnp.float32)
        for x in range(CX):
            packed = jnp.where(slot == x, roll(windy[x, pl.ds(k * ROWS, ROWS), :], 8 * x + 3), packed)
        to_n = jnp.where(inside == k, roll(packed, k - 2), to_n)
        to_s = jnp.where(inside == k, roll(packed, k - 3), to_s)
    wpack[0] = to_n
    wpack[1] = to_s
    for copy in wy_copies:
        copy.start()

    for s in range(NSC):
        for x in INNER_X:
            load_scalar(s, x).wait()

    def pack_first(k, carry):
        rows = rows_of(k)
        for pair in range(2):
            packs = []
            for s in (2 * pair, 2 * pair + 1):
                packed = jnp.zeros((ROWS, LANES), jnp.float32)
                for x in range(CX):
                    packed = jnp.where(slot == x, roll(field[0, H + x, s, rows, :], 8 * x + 3), packed)
                packs.append(packed)
            pack_send(0, k, pair, *packs)
        for copy in y_copies(0, k):
            copy.start()
        return carry

    lax.fori_loop(0, CHUNKS, pack_first, 0)

    load_map.wait()
    for x in range(CX):
        factor = jnp.broadcast_to(mapbuf[pl.ds(x, 1), :], (ROWS, LANES))
        minus = factor * factor
        square[0, x] = minus * (1.0 / 3.0)
        square[1, x] = minus * 0.5
        square[2, x] = minus
    for x in range(1, CX - 1):
        load_wind(0, x).wait()
    for copy in wx_copies:
        copy.wait_recv()
    for copy in wy_copies:
        copy.wait_recv()

    from_s = wgot[0]
    from_n = wgot[1]
    for k in range(CHUNKS):
        rows = pl.ds(k * ROWS, ROWS)
        for x in range(CX + 1):
            speed = (windx[x, rows, :] + windx[x + 1, rows, :]) * (1.0 / 120.0)
            facex[x, rows, :] = speed
            facex_abs[x, rows, :] = jnp.abs(speed)
        merged = jnp.where(low, roll(from_s, 2 - k), roll(from_n, 3 - k))
        for x in range(CX):
            centre = windy[x, rows, :]
            halo = roll(merged, -(8 * x + 3))
            left = (roll(jnp.where(lane == LANES - 1, halo, centre), 1) + centre) * (1.0 / 120.0)
            right = (roll(jnp.where(lane == 0, halo, centre), -1) + centre) * (1.0 / 120.0)
            face_l[x, rows, :] = left
            face_l_abs[x, rows, :] = jnp.abs(left)
            face_r[x, rows, :] = right
            face_r_abs[x, rows, :] = jnp.abs(right)

    size = NSC * ROWS
    half = CX // 2

    def section(sec, k, last):
        rows = rows_of(k)
        merged = []
        for pair in range(2):
            from_south, from_north = got_s[sec, k, pair], got_n[sec, k, pair]
            merged.append(jnp.where(low, from_south, roll(from_north, 3)))
            merged.append(jnp.where(low, roll(from_south, -3), from_north))
        merged = jnp.concatenate(merged, axis=0)
        for part in range(2):
            for x in range(part * half, (part + 1) * half):
                at = pl.ds(x * size, size)
                high, rest = split(field[sec, H + x, :, rows, :].reshape(size, LANES))
                cells[at, 0:LANES] = high
                cells[at, LANES : 2 * LANES] = rest
                high, rest = split(roll(merged, -(8 * x + 3)))
                cells[at, 2 * LANES : 3 * LANES] = high
                cells[at, 3 * LANES : 4 * LANES] = rest
            at = pl.ds(part * half * size, half * size)
            across[at, :] = jnp.dot(cells[at, :], stencil[...], preferred_element_type=jnp.float32)
        packs = []
        for s in range(NSC):
            packed = jnp.zeros((ROWS, LANES), jnp.float32)
            q, g, d2, d3, d4, even, flux = {}, {}, {}, {}, {}, {}, {}
            for i in range(CX + 2 * H):
                q[i] = field[sec, i, s, rows, :]
                if i >= 1:
                    g[i - 1] = q[i] - q[i - 1]
                if i >= 2:
                    d2[i - 1] = g[i - 1] - g[i - 2]
                if i >= 3:
                    d3[i - 2] = d2[i - 1] - d2[i - 2]
                if i >= 4:
                    d4[i - 2] = d3[i - 2] - d3[i - 3]
                    even[i - 2] = (d4[i - 2] - 5.0 * d2[i - 2]) + 30.0 * q[i - 2]
                if i >= 5:
                    f = i - 5
                    flux[f] = facex[f, rows, :] * (even[i - 3] + even[i - 2]) - facex_abs[f, rows, :] * (d4[i - 2] - d4[i - 3])
                if i >= 6:
                    x = i - 6
                    at = pl.ds(x * size + s * ROWS, ROWS)
                    total = flux[x + 1] - flux[x]
                    total += face_r[x, rows, :] * across[at, 0:LANES] - face_r_abs[x, rows, :] * across[at, LANES : 2 * LANES]
                    total -= face_l[x, rows, :] * across[at, 2 * LANES : 3 * LANES] - face_l_abs[x, rows, :] * across[at, 3 * LANES : 4 * LANES]
                    new = field[0, H + x, s, rows, :] - square[sec, x] * total
                    if last:
                        result[x, s, rows, :] = new
                    else:
                        field[sec + 1, H + x, s, rows, :] = new
                        packed = jnp.where(slot == x, roll(new, 8 * x + 3), packed)
            packs.append(packed)
        if not last:
            for pair in range(2):
                pack_send(sec + 1, k, pair, packs[2 * pair], packs[2 * pair + 1])

    def early(step, carry):
        sec, k = step // CHUNKS, lax.rem(step, CHUNKS)
        for copy in x_copies(sec, k) + y_copies(sec, k):
            copy.wait_recv()
        section(sec, k, False)
        for copy in x_copies(sec + 1, k) + y_copies(sec + 1, k):
            copy.start()
        return carry

    lax.fori_loop(0, 2 * CHUNKS, early, 0)

    def store(k):
        rows = rows_of(k)
        return pltpu.make_async_copy(result.at[:, :, rows, :], out.at[:, :, rows, :], store_o.at[k])

    def late(k, carry):
        for copy in x_copies(2, k) + y_copies(2, k):
            copy.wait_recv()
        section(2, k, True)
        store(k).start()
        return carry

    lax.fori_loop(0, CHUNKS, late, 0)

    for copy in wx_copies + wy_copies:
        copy.wait_send()

    def finish(step, carry):
        sec, k = step // CHUNKS, lax.rem(step, CHUNKS)
        for copy in x_copies(sec, k) + y_copies(sec, k):
            copy.wait_send()
        return carry

    lax.fori_loop(0, 3 * CHUNKS, finish, 0)

    def stored(k, carry):
        store(k).wait()
        return carry

    lax.fori_loop(0, CHUNKS, stored, 0)


def advance(scalars, winds, map_factor):
    f32 = jnp.float32
    dma = pltpu.SemaphoreType.DMA
    return pl.pallas_call(
        step_kernel,
        out_shape=jax.ShapeDtypeStruct((CX, NSC, LEV, LANES), f32),
        in_specs=[pl.BlockSpec(memory_space=pltpu.HBM)] * 3,
        out_specs=pl.BlockSpec(memory_space=pl.ANY),
        scratch_shapes=[
            pltpu.VMEM((3, CX + 2 * H, NSC, LEV, LANES), f32),
            pltpu.VMEM((CX + 2, LEV, LANES), f32),
            pltpu.VMEM((CX, LEV, LANES), f32),
            pltpu.VMEM((CX + 1, LEV, LANES), f32),
            pltpu.VMEM((CX + 1, LEV, LANES), f32),
            pltpu.VMEM((CX, LEV, LANES), f32),
            pltpu.VMEM((CX, LEV, LANES), f32),
            pltpu.VMEM((CX, LEV, LANES), f32),
            pltpu.VMEM((CX, LEV, LANES), f32),
            pltpu.VMEM((3, CX, ROWS, LANES), f32),
            pltpu.VMEM((3, CHUNKS, 2, ROWS, LANES), f32),
            pltpu.VMEM((3, CHUNKS, 2, ROWS, LANES), f32),
            pltpu.VMEM((3, CHUNKS, 2, ROWS, LANES), f32),
            pltpu.VMEM((3, CHUNKS, 2, ROWS, LANES), f32),
            pltpu.VMEM((CX, NSC, LEV, LANES), f32),
            pltpu.VMEM((2, ROWS, LANES), f32),
            pltpu.VMEM((2, ROWS, LANES), f32),
            pltpu.VMEM((CX, LANES), f32),
            pltpu.VMEM((4 * LANES, 4 * LANES), jnp.bfloat16),
            pltpu.VMEM((CX * NSC * ROWS, 4 * LANES), jnp.bfloat16),
            pltpu.VMEM((CX * NSC * ROWS, 4 * LANES), f32),
            dma((NSC, CX)),
            dma((2, CX)),
            dma(()),
            dma((3, CHUNKS, 2)),
            dma((3, CHUNKS, 2)),
            dma((3, CHUNKS, 2)),
            dma((3, CHUNKS, 2)),
            dma((2,)),
            dma((2,)),
            dma((2,)),
            dma((2,)),
            dma((CHUNKS,)),
        ],
        compiler_params=pltpu.CompilerParams(collective_id=0, has_side_effects=True, vmem_limit_bytes=58 << 20),
        name="advance",
    )(scalars, winds, map_factor)


def urban_kernel(
    adv, counts, cols, classes, table, wall, indoor, out, wall_out, indoor_out, body, low_in, low_out, heat_pad, sem_in, sem_low, sem_out
):
    load_low = pltpu.make_async_copy(adv.at[:, 0, pl.ds(0, LOW), :], low_in, sem_in)
    load_low.start()
    rest = []
    for x in range(CX):
        rest.append(pltpu.make_async_copy(adv.at[x, 0, pl.ds(LOW, LEV - LOW), :], out.at[0, pl.ds(LOW, LEV - LOW), x, :], sem_out.at[0, x]))
        for s in range(1, NSC):
            rest.append(pltpu.make_async_copy(adv.at[x, s], out.at[s, :, x, :], sem_out.at[s, x]))
    for copy in rest:
        copy.start()
    slots = cols.shape[1]
    column = cols[...]
    col_x = column // LANES
    col_y = column % LANES
    live = lax.broadcasted_iota(jnp.int32, (1, slots), 1) < counts[0]
    onehot = (lax.broadcasted_iota(jnp.int32, (LANES, slots), 0) == col_y).astype(jnp.float32)
    ncls = table.shape[0]
    picked = (lax.broadcasted_iota(jnp.int32, (ncls, slots), 0) == classes[...]).astype(jnp.float32)
    areas = lax.dot_general(
        table[...], picked, (((0,), (0,)), ((), ())), precision=lax.Precision.HIGHEST, preferred_element_type=jnp.float32
    )
    load_low.wait()
    gathered = jnp.dot(
        low_in[...].reshape(CX * LOW, LANES), onehot, precision=lax.Precision.HIGHEST, preferred_element_type=jnp.float32
    ).reshape(CX, LOW, slots)
    air = jnp.zeros((LOW, slots), jnp.float32)
    for x in range(CX):
        air = jnp.where(col_x == x, gathered[x], air)
    walls = wall[...]
    room = indoor[...]
    top = walls[0:1]
    heat = heat_coef * areas * (top - air[:UL])
    first = top - wall_coef * jnp.sum(heat, axis=0, keepdims=True) + conduct * (walls[1:2] - top)
    middle = walls[1:-1] + conduct * (walls[:-2] - 2.0 * walls[1:-1] + walls[2:])
    bottom = walls[NWL - 1 : NWL]
    last = bottom + conduct * (walls[NWL - 2 : NWL - 1] - bottom) + inner_coef * (room - bottom)
    wall_out[0:1] = jnp.where(live, first, top)
    wall_out[1 : NWL - 1] = jnp.where(live, middle, walls[1:-1])
    wall_out[NWL - 1 : NWL] = jnp.where(live, last, bottom)
    indoor_out[...] = jnp.where(live, room + room_coef * (bottom - room), room)
    heat_pad[...] = jnp.zeros_like(heat_pad)
    heat_pad[0:UL] = jnp.where(live, flux_coef * heat, 0.0)
    padded = heat_pad[...]
    for x in range(CX):
        body[x] = jnp.where(col_x == x, padded, 0.0)
    spread = lax.dot_general(
        body[...].reshape(CX * LOW, slots), onehot, (((1,), (1,)), ((), ())),
        precision=lax.Precision.HIGHEST, preferred_element_type=jnp.float32,
    )
    low_out[...] = low_in[...] + spread.reshape(CX, LOW, LANES)
    final = [pltpu.make_async_copy(low_out.at[x], out.at[0, pl.ds(0, LOW), x, :], sem_low.at[x]) for x in range(CX)]
    for copy in final:
        copy.start()
    for copy in rest + final:
        copy.wait()


def urban(adv, counts, cols, classes, table, wall, indoor):
    f32 = jnp.float32
    slots = wall.shape[1]
    vmem = pl.BlockSpec(memory_space=pltpu.VMEM)
    anywhere = pl.BlockSpec(memory_space=pl.ANY)
    dma = pltpu.SemaphoreType.DMA
    return pl.pallas_call(
        urban_kernel,
        out_shape=(
            jax.ShapeDtypeStruct((NSC, LEV, CX, LANES), f32),
            jax.ShapeDtypeStruct((NWL, slots), f32),
            jax.ShapeDtypeStruct((1, slots), f32),
        ),
        in_specs=[anywhere, pl.BlockSpec(memory_space=pltpu.SMEM)] + [vmem] * 5,
        out_specs=(anywhere, vmem, vmem),
        scratch_shapes=[
            pltpu.VMEM((CX, LOW, slots), f32),
            pltpu.VMEM((CX, LOW, LANES), f32),
            pltpu.VMEM((CX, LOW, LANES), f32),
            pltpu.VMEM((LOW, slots), f32),
            dma(()),
            dma((CX,)),
            dma((NSC, CX)),
        ],
        compiler_params=pltpu.CompilerParams(vmem_limit_bytes=16 << 20),
        name="urban",
    )(adv, counts, cols.reshape(1, slots), classes.reshape(1, slots), table, wall, indoor.reshape(1, slots))


def per_device(scalars, winds, map_factor, urban_counts, urban_cols, street_class, area_table, wall_temp, indoor_temp):
    adv = advance(scalars, winds, map_factor)
    scalars_out, wall_out, indoor_out = urban(
        adv, urban_counts, urban_cols, street_class, area_table, wall_temp, indoor_temp
    )
    return (scalars_out, wall_out, indoor_out.reshape(indoor_temp.shape))


def solution(mesh):
    in_specs = (
        P(None, None, "gx", "gy"),
        P(None, None, "gx", "gy"),
        P("gx", "gy"),
        P(("gx", "gy")),
        P(("gx", "gy")),
        P(("gx", "gy")),
        P(),
        P(None, ("gx", "gy")),
        P(("gx", "gy")),
    )
    out_specs = (P(None, None, "gx", "gy"), P(None, ("gx", "gy")), P(("gx", "gy")))
    return jax.shard_map(per_device, mesh=mesh, in_specs=in_specs, out_specs=out_specs, check_vma=False)
```

```python
import jax
import jax.numpy as jnp
from jax import lax
from jax.experimental import pallas as pl
from jax.experimental.pallas import tpu as pltpu
from jax.sharding import PartitionSpec as P

MESH = pl.DeviceIdType.MESH
UL = 10
NWL = 10
LOW = 16

heat_coef = 0.5
wall_coef = 0.05
conduct = 0.3
inner_coef = 0.2
room_coef = 0.1
flux_coef = 0.5

CX = 16
LANES = 128
NSC = 4
LEV = 64
ROWS = 8
CHUNKS = LEV // ROWS
STRIDE = LEV + ROWS
H = 3
EDGE_X = (0, 1, 2, 13, 14, 15)
INNER_X = tuple(range(3, 13))


def roll(value, shift):
    return pltpu.roll(value, shift % LANES, 1)


def split(value):
    high = value.astype(jnp.bfloat16)
    return high, (value - high.astype(jnp.float32)).astype(jnp.bfloat16)


def fill_stencil(stencil):
    row = lax.broadcasted_iota(jnp.int32, (LANES, LANES), 0)
    column = lax.broadcasted_iota(jnp.int32, (LANES, LANES), 1)
    for block in range(4):
        offset = row - column + (2 if block < 2 else 3)
        weights = (1.0, -8.0, 37.0, 37.0, -8.0, 1.0) if block % 2 == 0 else (-1.0, 5.0, -10.0, 10.0, -5.0, 1.0)
        band = jnp.zeros((LANES, LANES), jnp.float32)
        for at, weight in enumerate(weights):
            band = jnp.where(offset == at, weight, band)
        band = band.astype(jnp.bfloat16)
        for part in range(2):
            stencil[pl.ds(part * LANES, LANES), pl.ds(block * LANES, LANES)] = band


def urban(counts, cols, classes, table, wall, indoor, out, wall_out, indoor_out, body, heat_pad):
    slots = cols.shape[1]
    column = cols[...]
    col_x = column // LANES
    col_y = column % LANES
    live = lax.broadcasted_iota(jnp.int32, (1, slots), 1) < counts[0]
    onehot = (lax.broadcasted_iota(jnp.int32, (LANES, slots), 0) == col_y).astype(jnp.float32)
    ncls = table.shape[0]
    picked = (lax.broadcasted_iota(jnp.int32, (ncls, slots), 0) == classes[...]).astype(jnp.float32)
    areas = lax.dot_general(
        table[...], picked, (((0,), (0,)), ((), ())), precision=lax.Precision.HIGHEST, preferred_element_type=jnp.float32
    )
    lowest = out[:, 0, pl.ds(0, LOW), :]
    gathered = jnp.dot(
        lowest.reshape(CX * LOW, LANES), onehot, precision=lax.Precision.HIGHEST, preferred_element_type=jnp.float32
    ).reshape(CX, LOW, slots)
    air = jnp.zeros((LOW, slots), jnp.float32)
    for x in range(CX):
        air = jnp.where(col_x == x, gathered[x], air)
    walls = wall[...]
    room = indoor[...]
    top = walls[0:1]
    heat = heat_coef * areas * (top - air[:UL])
    first = top - wall_coef * jnp.sum(heat, axis=0, keepdims=True) + conduct * (walls[1:2] - top)
    middle = walls[1:-1] + conduct * (walls[:-2] - 2.0 * walls[1:-1] + walls[2:])
    bottom = walls[NWL - 1 : NWL]
    last = bottom + conduct * (walls[NWL - 2 : NWL - 1] - bottom) + inner_coef * (room - bottom)
    wall_out[0:1] = jnp.where(live, first, top)
    wall_out[1 : NWL - 1] = jnp.where(live, middle, walls[1:-1])
    wall_out[NWL - 1 : NWL] = jnp.where(live, last, bottom)
    indoor_out[...] = jnp.where(live, room + room_coef * (bottom - room), room)
    heat_pad[...] = jnp.zeros_like(heat_pad)
    heat_pad[0:UL] = jnp.where(live, flux_coef * heat, 0.0)
    padded = heat_pad[...]
    for x in range(CX):
        body[x] = jnp.where(col_x == x, padded, 0.0)
    spread = lax.dot_general(
        body[...].reshape(CX * LOW, slots), onehot, (((1,), (1,)), ((), ())),
        precision=lax.Precision.HIGHEST, preferred_element_type=jnp.float32,
    )
    out[:, 0, pl.ds(0, LOW), :] = out[:, 0, pl.ds(0, LOW), :] + spread.reshape(CX, LOW, LANES)


def step_kernel(
    scal, wind, mapf, counts, cols, classes, table, wall, indoor, out, wall_out, indoor_out,
    field0, field1, field2, windx, windy, facex, face_r, face_l, edge_weight, square, give_n, give_s, got_s, got_n,
    wpack, wgot, mapbuf, stencil, cells, across,
    load_s, load_w, load_m, sx, rx, sy, ry, swx, rwx, swy, rwy,
    cols_buf, classes_buf, table_buf, wall_buf, indoor_buf, spread_in, heat_pad, load_u,
):
    fields = (field0, field1, field2)
    gx, gy = lax.axis_index("gx"), lax.axis_index("gy")
    nx, ny = lax.axis_size("gx"), lax.axis_size("gy")
    east, west = {"gx": lax.rem(gx + 1, nx)}, {"gx": lax.rem(gx + nx - 1, nx)}
    north, south = {"gy": lax.rem(gy + 1, ny)}, {"gy": lax.rem(gy + ny - 1, ny)}

    barrier = pltpu.get_barrier_semaphore()
    for device in (east, west, north, south):
        pl.semaphore_signal(barrier, inc=1, device_id=device, device_id_type=MESH)

    def load_scalar(s, x):
        return pltpu.make_async_copy(scal.at[s, :, x, :], field0.at[H + x, s, pl.ds(0, LEV), :], load_s.at[s, x])

    def load_wind(which, x):
        target = (windx.at[1 + x] if which == 0 else windy.at[x]).at[pl.ds(0, LEV), :]
        return pltpu.make_async_copy(wind.at[which, :, x, :], target, load_w.at[which, x])

    load_map = pltpu.make_async_copy(mapf, mapbuf, load_m)
    for s in range(NSC):
        for x in EDGE_X:
            load_scalar(s, x).start()
    load_wind(0, 0).start()
    load_wind(0, CX - 1).start()
    for x in range(CX):
        load_wind(1, x).start()
    for s in range(NSC):
        for x in INNER_X:
            load_scalar(s, x).start()
    for x in range(1, CX - 1):
        load_wind(0, x).start()
    load_map.start()
    urban_loads = [
        pltpu.make_async_copy(source, target, load_u.at[n])
        for n, (source, target) in enumerate(
            ((cols, cols_buf), (classes, classes_buf), (table, table_buf), (wall, wall_buf), (indoor, indoor_buf))
        )
    ]
    for copy in urban_loads:
        copy.start()

    def remote(src, dst, send, recv, device):
        return pltpu.make_async_remote_copy(
            src_ref=src, dst_ref=dst, send_sem=send, recv_sem=recv, device_id=device, device_id_type=MESH
        )

    def rows_of(k):
        return pl.ds(pl.multiple_of(k * ROWS, ROWS), ROWS)

    def x_copies(sec, k):
        rows = rows_of(k)
        return (
            remote(fields[sec].at[pl.ds(CX, H), :, rows, :], fields[sec].at[pl.ds(0, H), :, rows, :],
                   sx.at[sec, k, 0], rx.at[sec, k, 0], east),
            remote(fields[sec].at[pl.ds(H, H), :, rows, :], fields[sec].at[pl.ds(CX + H, H), :, rows, :],
                   sx.at[sec, k, 1], rx.at[sec, k, 1], west),
        )

    def y_copies(sec, k):
        return (
            remote(give_n.at[sec, k], got_s.at[sec, k], sy.at[sec, k, 0], ry.at[sec, k, 0], north),
            remote(give_s.at[sec, k], got_n.at[sec, k], sy.at[sec, k, 1], ry.at[sec, k, 1], south),
        )

    wx_copies = (
        remote(windx.at[CX, pl.ds(0, LEV), :], windx.at[0, pl.ds(0, LEV), :], swx.at[0], rwx.at[0], east),
        remote(windx.at[1, pl.ds(0, LEV), :], windx.at[CX + 1, pl.ds(0, LEV), :], swx.at[1], rwx.at[1], west),
    )
    wy_copies = (
        remote(wpack.at[0], wgot.at[0], swy.at[0], rwy.at[0], north),
        remote(wpack.at[1], wgot.at[1], swy.at[1], rwy.at[1], south),
    )

    for s in range(NSC):
        for x in EDGE_X:
            load_scalar(s, x).wait()
    load_wind(0, 0).wait()
    load_wind(0, CX - 1).wait()
    pl.semaphore_wait(barrier, 4)
    for copy in wx_copies:
        copy.start()

    def send_first(k, carry):
        for copy in x_copies(0, k):
            copy.start()
        return carry

    lax.fori_loop(0, CHUNKS, send_first, 0)
    fill_stencil(stencil)

    lane = lax.broadcasted_iota(jnp.int32, (ROWS, LANES), 1)
    slot = lane // 8
    inside = lane % 8
    low = inside < 3

    def pack_send(sec, k, pair, first, second):
        give_n[sec, k, pair] = jnp.where(low, first, roll(second, 3))
        give_s[sec, k, pair] = jnp.where(low, roll(first, -3), second)

    for x in range(CX):
        load_wind(1, x).wait()
    to_n = jnp.zeros((ROWS, LANES), jnp.float32)
    to_s = jnp.zeros((ROWS, LANES), jnp.float32)
    lanes = lax.broadcasted_iota(jnp.int32, (LEV, LANES), 1) // 8
    packed = jnp.zeros((LEV, LANES), jnp.float32)
    for x in range(CX):
        packed = jnp.where(lanes == x, roll(windy[x, pl.ds(0, LEV), :], 8 * x + 3), packed)
    for k in range(CHUNKS):
        piece = packed[k * ROWS : (k + 1) * ROWS]
        to_n = jnp.where(inside == k, roll(piece, k - 2), to_n)
        to_s = jnp.where(inside == k, roll(piece, k - 3), to_s)
    wpack[0] = to_n
    wpack[1] = to_s
    for copy in wy_copies:
        copy.start()

    for s in range(NSC):
        for x in INNER_X:
            load_scalar(s, x).wait()

    many = lax.broadcasted_iota(jnp.int32, (NSC * ROWS, LANES), 1) // 8

    def pack_first(k, carry):
        rows = rows_of(k)
        packed = jnp.zeros((NSC * ROWS, LANES), jnp.float32)
        for x in range(CX):
            value = field0[H + x, :, rows, :].reshape(NSC * ROWS, LANES)
            packed = jnp.where(many == x, roll(value, 8 * x + 3), packed)
        for pair in range(2):
            at = 2 * pair * ROWS
            pack_send(0, k, pair, packed[at : at + ROWS], packed[at + ROWS : at + 2 * ROWS])
        for copy in y_copies(0, k):
            copy.start()
        return carry

    lax.fori_loop(0, CHUNKS, pack_first, 0)

    load_map.wait()
    for x in range(CX):
        factor = jnp.broadcast_to(mapbuf[pl.ds(x, 1), :], (ROWS, LANES))
        minus = factor * factor
        square[0, x] = minus * (1.0 / 3.0)
        square[1, x] = minus * 0.5
        square[2, x] = minus
    for x in range(1, CX - 1):
        load_wind(0, x).wait()
    for copy in wx_copies:
        copy.wait_recv()
    for copy in wy_copies:
        copy.wait_recv()

    from_s = wgot[0]
    from_n = wgot[1]
    half_levels = LEV // 2
    lanes = lax.broadcasted_iota(jnp.int32, (half_levels, LANES), 1)
    slots, within = lanes // 8, lanes % 8
    below = within < 3
    for part in range(2):
        rows = pl.ds(part * half_levels, half_levels)
        for x in range(CX + 1):
            facex[x, rows, :] = (windx[x, rows, :] + windx[x + 1, rows, :]) * (1.0 / 120.0)
        merged = jnp.concatenate(
            [
                jnp.where(low, roll(from_s, 2 - k), roll(from_n, 3 - k))
                for k in range(part * CHUNKS // 2, (part + 1) * CHUNKS // 2)
            ],
            axis=0,
        )
        zero = jnp.zeros((half_levels, LANES), jnp.float32)

        def faces(x, packed):
            left, right = packed
            centre = windy[x, rows, :]
            halo = roll(merged, -(8 * x + 3))
            behind = (roll(jnp.where(lanes == LANES - 1, halo, centre), 1) + centre) * (1.0 / 120.0)
            ahead = (roll(jnp.where(lanes == 0, halo, centre), -1) + centre) * (1.0 / 120.0)
            face_l[x, rows, :] = behind
            face_r[x, rows, :] = ahead
            return (
                jnp.where(slots == x, roll(behind, 8 * x + 3), left),
                jnp.where(slots == x, roll(ahead, 8 * x + 3), right),
            )

        left, right = zero, zero
        for x in range(CX):
            left, right = faces(x, (left, right))
        right_abs, left_abs = jnp.abs(right), jnp.abs(left)
        three = jnp.where(below, right - right_abs, jnp.where(within < 6, -(left + left_abs), zero))
        two = jnp.where(
            (within == 1) | (within == 2),
            (5.0 * right_abs - 8.0 * right) + (left_abs - left),
            jnp.where((within == 3) | (within == 4), (right + right_abs) + (8.0 * left + 5.0 * left_abs), zero),
        )
        one = jnp.where(
            within == 2,
            (37.0 * right - 10.0 * right_abs) + (8.0 * left - 5.0 * left_abs),
            jnp.where(within == 3, -(8.0 * right + 5.0 * right_abs) - (37.0 * left + 10.0 * left_abs), zero),
        )
        edge_weight[0, rows, :] = one
        edge_weight[1, rows, :] = two
        edge_weight[2, rows, :] = three

    size = NSC * ROWS
    half = CX // 2
    edge = (lane < H) | (lane >= LANES - H)

    def section(sec, k, last):
        rows = rows_of(k)
        for part in range(2):
            for x in range(part * half, (part + 1) * half):
                at = pl.ds(x * size, size)
                high, rest = split(fields[sec][H + x, :, rows, :].reshape(size, LANES))
                cells[at, 0:LANES] = high
                cells[at, LANES : 2 * LANES] = rest
            at = pl.ds(part * half * size, half * size)
            across[at, :] = jnp.dot(cells[at, :], stencil[...], preferred_element_type=jnp.float32)
        for pair in range(2):
            from_south, from_north = got_s[sec, k, pair], got_n[sec, k, pair]
            halos = (
                jnp.where(low, from_south, roll(from_north, 3)),
                jnp.where(low, roll(from_south, -3), from_north),
            )
            added = []
            for halo in halos:
                added.append(
                    sum(
                        edge_weight[r - 1, rows, :] * jnp.where(low, roll(halo, -r), roll(halo, r))
                        for r in (1, 2, 3)
                    )
                )
            members = (2 * pair, 2 * pair + 1)
            packs = {s: jnp.zeros((ROWS, LANES), jnp.float32) for s in members}
            q, g, d2, d3, d4, even, flux = ({s: {} for s in members} for _ in range(7))
            for i in range(CX + 2 * H):
                f, x = i - 5, i - 6
                if f >= 0:
                    speed = facex[f, rows, :]
                    speed_abs = jnp.abs(speed)
                if x >= 0:
                    ahead, behind, scale = face_r[x, rows, :], face_l[x, rows, :], square[sec, x]
                    ahead_abs, behind_abs = jnp.abs(ahead), jnp.abs(behind)
                for s in members:
                    q[s][i] = fields[sec][i, s, rows, :]
                    if i >= 1:
                        g[s][i - 1] = q[s][i] - q[s][i - 1]
                    if i >= 2:
                        d2[s][i - 1] = g[s][i - 1] - g[s][i - 2]
                    if i >= 3:
                        d3[s][i - 2] = d2[s][i - 1] - d2[s][i - 2]
                    if i >= 4:
                        d4[s][i - 2] = d3[s][i - 2] - d3[s][i - 3]
                        even[s][i - 2] = (d4[s][i - 2] - 5.0 * d2[s][i - 2]) + 30.0 * q[s][i - 2]
                    if f >= 0:
                        flux[s][f] = speed * (even[s][i - 3] + even[s][i - 2]) - speed_abs * (d4[s][i - 2] - d4[s][i - 3])
                    if x >= 0:
                        at = pl.ds(x * size + s * ROWS, ROWS)
                        total = flux[s][x + 1] - flux[s][x]
                        total += ahead * across[at, 0:LANES] - ahead_abs * across[at, LANES : 2 * LANES]
                        total -= behind * across[at, 2 * LANES : 3 * LANES] - behind_abs * across[at, 3 * LANES : 4 * LANES]
                        total += jnp.where(edge, roll(added[s % 2], -(8 * x + 3)), 0.0)
                        new = (field0[H + x, s, rows, :] if sec else q[s][H + x]) - scale * total
                        if last:
                            out[x, s, rows, :] = new
                        else:
                            fields[sec + 1][H + x, s, rows, :] = new
                            packs[s] = jnp.where(slot == x, roll(new, 8 * x + 3), packs[s])
            if not last:
                pack_send(sec + 1, k, pair, packs[members[0]], packs[members[1]])

    for sec in range(2):

        def early(k, carry, sec=sec):
            for copy in x_copies(sec, k) + y_copies(sec, k):
                copy.wait_recv()
            section(sec, k, False)
            for copy in x_copies(sec + 1, k) + y_copies(sec + 1, k):
                copy.start()
            return carry

        lax.fori_loop(0, CHUNKS, early, 0)

    def late(k, carry):
        for copy in x_copies(2, k) + y_copies(2, k):
            copy.wait_recv()
        section(2, k, True)

        @pl.when(k == LOW // ROWS - 1)
        def _():
            for copy in urban_loads:
                copy.wait()
            urban(counts, cols_buf, classes_buf, table_buf, wall_buf, indoor_buf, out, wall_out, indoor_out, spread_in, heat_pad)

        return carry

    lax.fori_loop(0, CHUNKS, late, 0)

    for copy in wx_copies + wy_copies:
        copy.wait_send()

    def finish(k, carry):
        for sec in range(3):
            for copy in x_copies(sec, k) + y_copies(sec, k):
                copy.wait_send()
        return carry

    lax.fori_loop(0, CHUNKS, finish, 0)


def advance(scalars, winds, map_factor, counts, cols, classes, table, wall, indoor):
    f32, i32 = jnp.float32, jnp.int32
    dma = pltpu.SemaphoreType.DMA
    slots = wall.shape[1]
    vmem = pl.BlockSpec(memory_space=pltpu.VMEM)
    anywhere = pl.BlockSpec(memory_space=pl.ANY)
    grids = (scalars, winds, map_factor)
    columns = (cols.reshape(1, slots), classes.reshape(1, slots), table, wall, indoor.reshape(1, slots))
    operands = [pltpu.with_memory_space_constraint(array, pltpu.HBM) for array in grids + columns]
    operands.insert(len(grids), counts)
    return pl.pallas_call(
        step_kernel,
        out_shape=(
            jax.ShapeDtypeStruct((CX, NSC, LEV, LANES), f32),
            jax.ShapeDtypeStruct((NWL, slots), f32),
            jax.ShapeDtypeStruct((1, slots), f32),
        ),
        in_specs=[anywhere] * 3 + [pl.BlockSpec(memory_space=pltpu.SMEM)] + [anywhere] * 5,
        out_specs=(vmem, vmem, vmem),
        scratch_shapes=[
            pltpu.VMEM((CX + 2 * H, NSC, STRIDE, LANES), f32),
            pltpu.VMEM((CX + 2 * H, NSC, STRIDE, LANES), f32),
            pltpu.VMEM((CX + 2 * H, NSC, STRIDE, LANES), f32),
            pltpu.VMEM((CX + 2, STRIDE, LANES), f32),
            pltpu.VMEM((CX, STRIDE, LANES), f32),
            pltpu.VMEM((CX + 1, STRIDE, LANES), f32),
            pltpu.VMEM((CX, STRIDE, LANES), f32),
            pltpu.VMEM((CX, STRIDE, LANES), f32),
            pltpu.VMEM((H, LEV, LANES), f32),
            pltpu.VMEM((3, CX, ROWS, LANES), f32),
            pltpu.VMEM((3, CHUNKS, 2, ROWS, LANES), f32),
            pltpu.VMEM((3, CHUNKS, 2, ROWS, LANES), f32),
            pltpu.VMEM((3, CHUNKS, 2, ROWS, LANES), f32),
            pltpu.VMEM((3, CHUNKS, 2, ROWS, LANES), f32),
            pltpu.VMEM((2, ROWS, LANES), f32),
            pltpu.VMEM((2, ROWS, LANES), f32),
            pltpu.VMEM((CX, LANES), f32),
            pltpu.VMEM((2 * LANES, 4 * LANES), jnp.bfloat16),
            pltpu.VMEM((CX * NSC * ROWS, 2 * LANES), jnp.bfloat16),
            pltpu.VMEM((CX * NSC * ROWS, 4 * LANES), f32),
            dma((NSC, CX)),
            dma((2, CX)),
            dma(()),
            dma((3, CHUNKS, 2)),
            dma((3, CHUNKS, 2)),
            dma((3, CHUNKS, 2)),
            dma((3, CHUNKS, 2)),
            dma((2,)),
            dma((2,)),
            dma((2,)),
            dma((2,)),
            pltpu.VMEM((1, slots), i32),
            pltpu.VMEM((1, slots), i32),
            pltpu.VMEM(table.shape, f32),
            pltpu.VMEM((NWL, slots), f32),
            pltpu.VMEM((1, slots), f32),
            pltpu.VMEM((CX, LOW, slots), f32),
            pltpu.VMEM((LOW, slots), f32),
            dma((5,)),
        ],
        compiler_params=pltpu.CompilerParams(collective_id=0, has_side_effects=True, vmem_limit_bytes=32 << 20),
        name="advance",
    )(*operands)


def store_kernel(adv, wall, indoor, out, wall_out, indoor_out, sem, sem_wall, sem_indoor):
    copies = [
        pltpu.make_async_copy(adv.at[x, s], out.at[s, :, x, :], sem.at[s, x]) for s in range(NSC) for x in range(CX)
    ]
    copies.append(pltpu.make_async_copy(wall, wall_out, sem_wall))
    copies.append(pltpu.make_async_copy(indoor, indoor_out, sem_indoor))
    for copy in copies:
        copy.start()
    for copy in copies:
        copy.wait()


def store(adv, wall, indoor):
    f32 = jnp.float32
    anywhere = pl.BlockSpec(memory_space=pl.ANY)
    dma = pltpu.SemaphoreType.DMA
    return pl.pallas_call(
        store_kernel,
        out_shape=(
            jax.ShapeDtypeStruct((NSC, LEV, CX, LANES), f32),
            jax.ShapeDtypeStruct(wall.shape, f32),
            jax.ShapeDtypeStruct(indoor.shape, f32),
        ),
        in_specs=[anywhere] * 3,
        out_specs=(anywhere,) * 3,
        scratch_shapes=[dma((NSC, CX)), dma(()), dma(())],
        compiler_params=pltpu.CompilerParams(vmem_limit_bytes=4 << 20),
        name="store",
    )(adv, wall, indoor)


def per_device(scalars, winds, map_factor, urban_counts, urban_cols, street_class, area_table, wall_temp, indoor_temp):
    adv, walls, rooms = advance(
        scalars, winds, map_factor, urban_counts, urban_cols, street_class, area_table, wall_temp, indoor_temp
    )
    scalars_out, wall_out, indoor_out = store(adv, walls, rooms)
    return (scalars_out, wall_out, indoor_out.reshape(indoor_temp.shape))


def solution(mesh):
    in_specs = (
        P(None, None, "gx", "gy"),
        P(None, None, "gx", "gy"),
        P("gx", "gy"),
        P(("gx", "gy")),
        P(("gx", "gy")),
        P(("gx", "gy")),
        P(),
        P(None, ("gx", "gy")),
        P(("gx", "gy")),
    )
    out_specs = (P(None, None, "gx", "gy"), P(None, ("gx", "gy")), P(("gx", "gy")))
    return jax.shard_map(per_device, mesh=mesh, in_specs=in_specs, out_specs=out_specs, check_vma=False)
```

```python
import jax
import jax.numpy as jnp
from jax import lax
from jax.experimental import pallas as pl
from jax.experimental.pallas import tpu as pltpu
from jax.sharding import PartitionSpec as P

MESH = pl.DeviceIdType.MESH
UL = 10
NWL = 10
LOW = 16

heat_coef = 0.5
wall_coef = 0.05
conduct = 0.3
inner_coef = 0.2
room_coef = 0.1
flux_coef = 0.5

CX = 16
LANES = 128
NSC = 4
LEV = 64
ROWS = 8
CHUNKS = LEV // ROWS
STRIDE = LEV + ROWS
FIRST = 2
H = 3
EDGE_X = (0, 1, 2, 13, 14, 15)
INNER_X = tuple(range(3, 13))


def roll(value, shift):
    return pltpu.roll(value, shift % LANES, 1)


def split(value):
    high = value.astype(jnp.bfloat16)
    return high, (value - high.astype(jnp.float32)).astype(jnp.bfloat16)


def fill_stencil(stencil):
    row = lax.broadcasted_iota(jnp.int32, (LANES, LANES), 0)
    column = lax.broadcasted_iota(jnp.int32, (LANES, LANES), 1)
    for block in range(4):
        offset = row - column + (2 if block < 2 else 3)
        weights = (1.0, -8.0, 37.0, 37.0, -8.0, 1.0) if block % 2 == 0 else (-1.0, 5.0, -10.0, 10.0, -5.0, 1.0)
        band = jnp.zeros((LANES, LANES), jnp.float32)
        for at, weight in enumerate(weights):
            band = jnp.where(offset == at, weight, band)
        band = band.astype(jnp.bfloat16)
        for part in range(2):
            stencil[pl.ds(part * LANES, LANES), pl.ds(block * LANES, LANES)] = band


def urban(counts, cols, classes, table, wall, indoor, out, wall_out, indoor_out, body, heat_pad):
    slots = cols.shape[1]
    column = cols[...]
    col_x = column // LANES
    col_y = column % LANES
    live = lax.broadcasted_iota(jnp.int32, (1, slots), 1) < counts[0]
    onehot = (lax.broadcasted_iota(jnp.int32, (LANES, slots), 0) == col_y).astype(jnp.float32)
    ncls = table.shape[0]
    picked = (lax.broadcasted_iota(jnp.int32, (ncls, slots), 0) == classes[...]).astype(jnp.float32)
    areas = lax.dot_general(
        table[...], picked, (((0,), (0,)), ((), ())), precision=lax.Precision.HIGHEST, preferred_element_type=jnp.float32
    )
    lowest = out[:, 0, pl.ds(0, LOW), :]
    gathered = jnp.dot(
        lowest.reshape(CX * LOW, LANES), onehot, precision=lax.Precision.HIGHEST, preferred_element_type=jnp.float32
    ).reshape(CX, LOW, slots)
    air = jnp.zeros((LOW, slots), jnp.float32)
    for x in range(CX):
        air = jnp.where(col_x == x, gathered[x], air)
    walls = wall[...]
    room = indoor[...]
    top = walls[0:1]
    heat = heat_coef * areas * (top - air[:UL])
    first = top - wall_coef * jnp.sum(heat, axis=0, keepdims=True) + conduct * (walls[1:2] - top)
    middle = walls[1:-1] + conduct * (walls[:-2] - 2.0 * walls[1:-1] + walls[2:])
    bottom = walls[NWL - 1 : NWL]
    last = bottom + conduct * (walls[NWL - 2 : NWL - 1] - bottom) + inner_coef * (room - bottom)
    wall_out[0:1] = jnp.where(live, first, top)
    wall_out[1 : NWL - 1] = jnp.where(live, middle, walls[1:-1])
    wall_out[NWL - 1 : NWL] = jnp.where(live, last, bottom)
    indoor_out[...] = jnp.where(live, room + room_coef * (bottom - room), room)
    heat_pad[...] = jnp.zeros_like(heat_pad)
    heat_pad[0:UL] = jnp.where(live, flux_coef * heat, 0.0)
    padded = heat_pad[...]
    for x in range(CX):
        body[x] = jnp.where(col_x == x, padded, 0.0)
    spread = lax.dot_general(
        body[...].reshape(CX * LOW, slots), onehot, (((1,), (1,)), ((), ())),
        precision=lax.Precision.HIGHEST, preferred_element_type=jnp.float32,
    )
    out[:, 0, pl.ds(0, LOW), :] = out[:, 0, pl.ds(0, LOW), :] + spread.reshape(CX, LOW, LANES)


def step_kernel(
    scal, wind, mapf, counts, cols, classes, table, wall, indoor, out, wall_out, indoor_out,
    field0, field1, field2, windx, windy, facex, face_r, face_l, edge_weight, square, give_n, give_s, got_s, got_n,
    wpack, wgot, mapbuf, stencil, cells, across,
    load_s, load_w, load_m, sx, rx, sy, ry, swx, rwx, swy, rwy,
    cols_buf, classes_buf, table_buf, wall_buf, indoor_buf, spread_in, heat_pad, load_u,
):
    fields = (field0, field1, field2)
    gx, gy = lax.axis_index("gx"), lax.axis_index("gy")
    nx, ny = lax.axis_size("gx"), lax.axis_size("gy")
    east, west = {"gx": lax.rem(gx + 1, nx)}, {"gx": lax.rem(gx + nx - 1, nx)}
    north, south = {"gy": lax.rem(gy + 1, ny)}, {"gy": lax.rem(gy + ny - 1, ny)}

    barrier = pltpu.get_barrier_semaphore()
    for device in (east, west, north, south):
        pl.semaphore_signal(barrier, inc=1, device_id=device, device_id_type=MESH)

    def load_scalar(s, x):
        return pltpu.make_async_copy(scal.at[s, :, x, :], field0.at[H + x, s, pl.ds(0, LEV), :], load_s.at[s, x])

    def load_wind(which, x):
        target = (windx.at[1 + x] if which == 0 else windy.at[x]).at[pl.ds(0, LEV), :]
        return pltpu.make_async_copy(wind.at[which, :, x, :], target, load_w.at[which, x])

    load_map = pltpu.make_async_copy(mapf, mapbuf, load_m)
    for s in range(NSC):
        for x in EDGE_X:
            load_scalar(s, x).start()
    load_wind(0, 0).start()
    load_wind(0, CX - 1).start()
    for x in range(CX):
        load_wind(1, x).start()
    for s in range(NSC):
        for x in INNER_X:
            load_scalar(s, x).start()
    for x in range(1, CX - 1):
        load_wind(0, x).start()
    load_map.start()
    urban_loads = [
        pltpu.make_async_copy(source, target, load_u.at[n])
        for n, (source, target) in enumerate(
            ((cols, cols_buf), (classes, classes_buf), (table, table_buf), (wall, wall_buf), (indoor, indoor_buf))
        )
    ]
    for copy in urban_loads:
        copy.start()

    def remote(src, dst, send, recv, device):
        return pltpu.make_async_remote_copy(
            src_ref=src, dst_ref=dst, send_sem=send, recv_sem=recv, device_id=device, device_id_type=MESH
        )

    def rows_of(k):
        return pl.ds(pl.multiple_of(k * ROWS, ROWS), ROWS)

    def x_copies(sec, k):
        rows = rows_of(k)
        return (
            remote(fields[sec].at[pl.ds(CX, H), :, rows, :], fields[sec].at[pl.ds(0, H), :, rows, :],
                   sx.at[sec, k, 0], rx.at[sec, k, 0], east),
            remote(fields[sec].at[pl.ds(H, H), :, rows, :], fields[sec].at[pl.ds(CX + H, H), :, rows, :],
                   sx.at[sec, k, 1], rx.at[sec, k, 1], west),
        )

    def y_copies(sec, k):
        return (
            remote(give_n.at[sec, k], got_s.at[sec, k], sy.at[sec, k, 0], ry.at[sec, k, 0], north),
            remote(give_s.at[sec, k], got_n.at[sec, k], sy.at[sec, k, 1], ry.at[sec, k, 1], south),
        )

    wx_copies = (
        remote(windx.at[CX, pl.ds(0, LEV), :], windx.at[0, pl.ds(0, LEV), :], swx.at[0], rwx.at[0], east),
        remote(windx.at[1, pl.ds(0, LEV), :], windx.at[CX + 1, pl.ds(0, LEV), :], swx.at[1], rwx.at[1], west),
    )
    wy_copies = (
        remote(wpack.at[0], wgot.at[0], swy.at[0], rwy.at[0], north),
        remote(wpack.at[1], wgot.at[1], swy.at[1], rwy.at[1], south),
    )

    for s in range(NSC):
        for x in EDGE_X:
            load_scalar(s, x).wait()
    load_wind(0, 0).wait()
    load_wind(0, CX - 1).wait()
    pl.semaphore_wait(barrier, 4)
    for copy in wx_copies:
        copy.start()

    def send_first(k, carry):
        for copy in x_copies(0, k):
            copy.start()
        return carry

    lax.fori_loop(0, FIRST, send_first, 0)

    lane = lax.broadcasted_iota(jnp.int32, (ROWS, LANES), 1)
    slot = lane // 8
    inside = lane % 8
    low = inside < 3

    def pack_send(sec, k, pair, first, second):
        give_n[sec, k, pair] = jnp.where(low, first, roll(second, 3))
        give_s[sec, k, pair] = jnp.where(low, roll(first, -3), second)

    for x in range(CX):
        load_wind(1, x).wait()
    to_n = jnp.zeros((ROWS, LANES), jnp.float32)
    to_s = jnp.zeros((ROWS, LANES), jnp.float32)
    lanes = lax.broadcasted_iota(jnp.int32, (LEV, LANES), 1) // 8
    packed = jnp.zeros((LEV, LANES), jnp.float32)
    for x in range(CX):
        packed = jnp.where(lanes == x, roll(windy[x, pl.ds(0, LEV), :], 8 * x + 3), packed)
    for k in range(CHUNKS):
        piece = packed[k * ROWS : (k + 1) * ROWS]
        to_n = jnp.where(inside == k, roll(piece, k - 2), to_n)
        to_s = jnp.where(inside == k, roll(piece, k - 3), to_s)
    wpack[0] = to_n
    wpack[1] = to_s
    for copy in wy_copies:
        copy.start()

    for s in range(NSC):
        for x in INNER_X:
            load_scalar(s, x).wait()

    many = lax.broadcasted_iota(jnp.int32, (NSC * ROWS, LANES), 1) // 8

    def pack_first(k, carry):
        rows = rows_of(k)
        packed = jnp.zeros((NSC * ROWS, LANES), jnp.float32)
        for x in range(CX):
            value = field0[H + x, :, rows, :].reshape(NSC * ROWS, LANES)
            packed = jnp.where(many == x, roll(value, 8 * x + 3), packed)
        for pair in range(2):
            at = 2 * pair * ROWS
            pack_send(0, k, pair, packed[at : at + ROWS], packed[at + ROWS : at + 2 * ROWS])
        for copy in y_copies(0, k):
            copy.start()

        @pl.when(k >= FIRST)
        def _():
            send_first(k, carry)

        return carry

    lax.fori_loop(0, CHUNKS, pack_first, 0)
    fill_stencil(stencil)

    load_map.wait()
    for x in range(CX):
        factor = jnp.broadcast_to(mapbuf[pl.ds(x, 1), :], (ROWS, LANES))
        minus = factor * factor
        square[0, x] = minus * (1.0 / 3.0)
        square[1, x] = minus * 0.5
        square[2, x] = minus
    for x in range(1, CX - 1):
        load_wind(0, x).wait()
    for copy in wx_copies:
        copy.wait_recv()
    for copy in wy_copies:
        copy.wait_recv()

    from_s = wgot[0]
    from_n = wgot[1]
    half_levels = LEV // 2
    lanes = lax.broadcasted_iota(jnp.int32, (half_levels, LANES), 1)
    slots, within = lanes // 8, lanes % 8
    below = within < 3
    for part in range(2):
        rows = pl.ds(part * half_levels, half_levels)
        for x in range(CX + 1):
            facex[x, rows, :] = (windx[x, rows, :] + windx[x + 1, rows, :]) * (1.0 / 120.0)
        merged = jnp.concatenate(
            [
                jnp.where(low, roll(from_s, 2 - k), roll(from_n, 3 - k))
                for k in range(part * CHUNKS // 2, (part + 1) * CHUNKS // 2)
            ],
            axis=0,
        )
        zero = jnp.zeros((half_levels, LANES), jnp.float32)

        def faces(x, packed):
            left, right = packed
            centre = windy[x, rows, :]
            halo = roll(merged, -(8 * x + 3))
            behind = (roll(jnp.where(lanes == LANES - 1, halo, centre), 1) + centre) * (1.0 / 120.0)
            ahead = (roll(jnp.where(lanes == 0, halo, centre), -1) + centre) * (1.0 / 120.0)
            face_l[x, rows, :] = behind
            face_r[x, rows, :] = ahead
            return (
                jnp.where(slots == x, roll(behind, 8 * x + 3), left),
                jnp.where(slots == x, roll(ahead, 8 * x + 3), right),
            )

        left, right = zero, zero
        for x in range(CX):
            left, right = faces(x, (left, right))
        right_abs, left_abs = jnp.abs(right), jnp.abs(left)
        three = jnp.where(below, right - right_abs, jnp.where(within < 6, -(left + left_abs), zero))
        two = jnp.where(
            (within == 1) | (within == 2),
            (5.0 * right_abs - 8.0 * right) + (left_abs - left),
            jnp.where((within == 3) | (within == 4), (right + right_abs) + (8.0 * left + 5.0 * left_abs), zero),
        )
        one = jnp.where(
            within == 2,
            (37.0 * right - 10.0 * right_abs) + (8.0 * left - 5.0 * left_abs),
            jnp.where(within == 3, -(8.0 * right + 5.0 * right_abs) - (37.0 * left + 10.0 * left_abs), zero),
        )
        edge_weight[0, rows, :] = one
        edge_weight[1, rows, :] = two
        edge_weight[2, rows, :] = three

    size = NSC * ROWS
    half = CX // 2
    edge = (lane < H) | (lane >= LANES - H)

    def section(sec, k, last):
        rows = rows_of(k)
        for part in range(2):
            for x in range(part * half, (part + 1) * half):
                at = pl.ds(x * size, size)
                high, rest = split(fields[sec][H + x, :, rows, :].reshape(size, LANES))
                cells[at, 0:LANES] = high
                cells[at, LANES : 2 * LANES] = rest
            at = pl.ds(part * half * size, half * size)
            across[at, :] = jnp.dot(cells[at, :], stencil[...], preferred_element_type=jnp.float32)
        for pair in range(2):
            from_south, from_north = got_s[sec, k, pair], got_n[sec, k, pair]
            halos = (
                jnp.where(low, from_south, roll(from_north, 3)),
                jnp.where(low, roll(from_south, -3), from_north),
            )
            added = []
            for halo in halos:
                added.append(
                    sum(
                        edge_weight[r - 1, rows, :] * jnp.where(low, roll(halo, -r), roll(halo, r))
                        for r in (1, 2, 3)
                    )
                )
            members = (2 * pair, 2 * pair + 1)
            packs = {s: jnp.zeros((ROWS, LANES), jnp.float32) for s in members}
            q, g, d2, d3, d4, even, flux = ({s: {} for s in members} for _ in range(7))
            for i in range(CX + 2 * H):
                f, x = i - 5, i - 6
                if f >= 0:
                    speed = facex[f, rows, :]
                    speed_abs = jnp.abs(speed)
                if x >= 0:
                    ahead, behind, scale = face_r[x, rows, :], face_l[x, rows, :], square[sec, x]
                    ahead_abs, behind_abs = jnp.abs(ahead), jnp.abs(behind)
                for s in members:
                    q[s][i] = fields[sec][i, s, rows, :]
                    if i >= 1:
                        g[s][i - 1] = q[s][i] - q[s][i - 1]
                    if i >= 2:
                        d2[s][i - 1] = g[s][i - 1] - g[s][i - 2]
                    if i >= 3:
                        d3[s][i - 2] = d2[s][i - 1] - d2[s][i - 2]
                    if i >= 4:
                        d4[s][i - 2] = d3[s][i - 2] - d3[s][i - 3]
                        even[s][i - 2] = (d4[s][i - 2] - 5.0 * d2[s][i - 2]) + 30.0 * q[s][i - 2]
                    if f >= 0:
                        flux[s][f] = speed * (even[s][i - 3] + even[s][i - 2]) - speed_abs * (d4[s][i - 2] - d4[s][i - 3])
                    if x >= 0:
                        at = pl.ds(x * size + s * ROWS, ROWS)
                        total = flux[s][x + 1] - flux[s][x]
                        total += ahead * across[at, 0:LANES] - ahead_abs * across[at, LANES : 2 * LANES]
                        total -= behind * across[at, 2 * LANES : 3 * LANES] - behind_abs * across[at, 3 * LANES : 4 * LANES]
                        total += jnp.where(edge, roll(added[s % 2], -(8 * x + 3)), 0.0)
                        new = (field0[H + x, s, rows, :] if sec else q[s][H + x]) - scale * total
                        if last:
                            out[x, s, rows, :] = new
                        else:
                            fields[sec + 1][H + x, s, rows, :] = new
                            packs[s] = jnp.where(slot == x, roll(new, 8 * x + 3), packs[s])
            if not last:
                pack_send(sec + 1, k, pair, packs[members[0]], packs[members[1]])

    for sec in range(2):

        def early(k, carry, sec=sec):
            for copy in x_copies(sec, k) + y_copies(sec, k):
                copy.wait_recv()
            section(sec, k, False)
            for copy in y_copies(sec + 1, k) + x_copies(sec + 1, k):
                copy.start()
            return carry

        lax.fori_loop(0, CHUNKS, early, 0)

    def late(k, carry):
        for copy in x_copies(2, k) + y_copies(2, k):
            copy.wait_recv()
        section(2, k, True)

        @pl.when(k == LOW // ROWS - 1)
        def _():
            for copy in urban_loads:
                copy.wait()
            urban(counts, cols_buf, classes_buf, table_buf, wall_buf, indoor_buf, out, wall_out, indoor_out, spread_in, heat_pad)

        return carry

    lax.fori_loop(0, CHUNKS, late, 0)

    for copy in wx_copies + wy_copies:
        copy.wait_send()

    def finish(k, carry):
        for sec in range(3):
            for copy in x_copies(sec, k) + y_copies(sec, k):
                copy.wait_send()
        return carry

    lax.fori_loop(0, CHUNKS, finish, 0)


def advance(scalars, winds, map_factor, counts, cols, classes, table, wall, indoor):
    f32, i32 = jnp.float32, jnp.int32
    dma = pltpu.SemaphoreType.DMA
    slots = wall.shape[1]
    vmem = pl.BlockSpec(memory_space=pltpu.VMEM)
    anywhere = pl.BlockSpec(memory_space=pl.ANY)
    grids = (scalars, winds, map_factor)
    columns = (cols.reshape(1, slots), classes.reshape(1, slots), table, wall, indoor.reshape(1, slots))
    operands = [pltpu.with_memory_space_constraint(array, pltpu.HBM) for array in grids + columns]
    operands.insert(len(grids), counts)
    return pl.pallas_call(
        step_kernel,
        out_shape=(
            jax.ShapeDtypeStruct((CX, NSC, LEV, LANES), f32),
            jax.ShapeDtypeStruct((NWL, slots), f32),
            jax.ShapeDtypeStruct((1, slots), f32),
        ),
        in_specs=[anywhere] * 3 + [pl.BlockSpec(memory_space=pltpu.SMEM)] + [anywhere] * 5,
        out_specs=(vmem, vmem, vmem),
        scratch_shapes=[
            pltpu.VMEM((CX + 2 * H, NSC, STRIDE, LANES), f32),
            pltpu.VMEM((CX + 2 * H, NSC, STRIDE, LANES), f32),
            pltpu.VMEM((CX + 2 * H, NSC, STRIDE, LANES), f32),
            pltpu.VMEM((CX + 2, STRIDE, LANES), f32),
            pltpu.VMEM((CX, STRIDE, LANES), f32),
            pltpu.VMEM((CX + 1, STRIDE, LANES), f32),
            pltpu.VMEM((CX, STRIDE, LANES), f32),
            pltpu.VMEM((CX, STRIDE, LANES), f32),
            pltpu.VMEM((H, LEV, LANES), f32),
            pltpu.VMEM((3, CX, ROWS, LANES), f32),
            pltpu.VMEM((3, CHUNKS, 2, ROWS, LANES), f32),
            pltpu.VMEM((3, CHUNKS, 2, ROWS, LANES), f32),
            pltpu.VMEM((3, CHUNKS, 2, ROWS, LANES), f32),
            pltpu.VMEM((3, CHUNKS, 2, ROWS, LANES), f32),
            pltpu.VMEM((2, ROWS, LANES), f32),
            pltpu.VMEM((2, ROWS, LANES), f32),
            pltpu.VMEM((CX, LANES), f32),
            pltpu.VMEM((2 * LANES, 4 * LANES), jnp.bfloat16),
            pltpu.VMEM((CX * NSC * ROWS, 2 * LANES), jnp.bfloat16),
            pltpu.VMEM((CX * NSC * ROWS, 4 * LANES), f32),
            dma((NSC, CX)),
            dma((2, CX)),
            dma(()),
            dma((3, CHUNKS, 2)),
            dma((3, CHUNKS, 2)),
            dma((3, CHUNKS, 2)),
            dma((3, CHUNKS, 2)),
            dma((2,)),
            dma((2,)),
            dma((2,)),
            dma((2,)),
            pltpu.VMEM((1, slots), i32),
            pltpu.VMEM((1, slots), i32),
            pltpu.VMEM(table.shape, f32),
            pltpu.VMEM((NWL, slots), f32),
            pltpu.VMEM((1, slots), f32),
            pltpu.VMEM((CX, LOW, slots), f32),
            pltpu.VMEM((LOW, slots), f32),
            dma((5,)),
        ],
        compiler_params=pltpu.CompilerParams(collective_id=0, has_side_effects=True, vmem_limit_bytes=32 << 20),
        name="advance",
    )(*operands)


def store_kernel(adv, wall, indoor, out, wall_out, indoor_out, sem, sem_wall, sem_indoor):
    copies = [
        pltpu.make_async_copy(adv.at[x, s], out.at[s, :, x, :], sem.at[s, x]) for s in range(NSC) for x in range(CX)
    ]
    copies.append(pltpu.make_async_copy(wall, wall_out, sem_wall))
    copies.append(pltpu.make_async_copy(indoor, indoor_out, sem_indoor))
    for copy in copies:
        copy.start()
    for copy in copies:
        copy.wait()


def store(adv, wall, indoor):
    f32 = jnp.float32
    anywhere = pl.BlockSpec(memory_space=pl.ANY)
    dma = pltpu.SemaphoreType.DMA
    return pl.pallas_call(
        store_kernel,
        out_shape=(
            jax.ShapeDtypeStruct((NSC, LEV, CX, LANES), f32),
            jax.ShapeDtypeStruct(wall.shape, f32),
            jax.ShapeDtypeStruct(indoor.shape, f32),
        ),
        in_specs=[anywhere] * 3,
        out_specs=(anywhere,) * 3,
        scratch_shapes=[dma((NSC, CX)), dma(()), dma(())],
        compiler_params=pltpu.CompilerParams(vmem_limit_bytes=4 << 20),
        name="store",
    )(adv, wall, indoor)


def per_device(scalars, winds, map_factor, urban_counts, urban_cols, street_class, area_table, wall_temp, indoor_temp):
    adv, walls, rooms = advance(
        scalars, winds, map_factor, urban_counts, urban_cols, street_class, area_table, wall_temp, indoor_temp
    )
    scalars_out, wall_out, indoor_out = store(adv, walls, rooms)
    return (scalars_out, wall_out, indoor_out.reshape(indoor_temp.shape))


def solution(mesh):
    in_specs = (
        P(None, None, "gx", "gy"),
        P(None, None, "gx", "gy"),
        P("gx", "gy"),
        P(("gx", "gy")),
        P(("gx", "gy")),
        P(("gx", "gy")),
        P(),
        P(None, ("gx", "gy")),
        P(("gx", "gy")),
    )
    out_specs = (P(None, None, "gx", "gy"), P(None, ("gx", "gy")), P(("gx", "gy")))
    return jax.shard_map(per_device, mesh=mesh, in_specs=in_specs, out_specs=out_specs, check_vma=False)
```

```python
import jax
import jax.numpy as jnp
from jax import lax
from jax.experimental import pallas as pl
from jax.experimental.pallas import tpu as pltpu
from jax.sharding import PartitionSpec as P

MESH = pl.DeviceIdType.MESH
UL = 10
NWL = 10
LOW = 16

heat_coef = 0.5
wall_coef = 0.05
conduct = 0.3
inner_coef = 0.2
room_coef = 0.1
flux_coef = 0.5

CX = 16
LANES = 128
NSC = 4
LEV = 64
ROWS = 8
CHUNKS = LEV // ROWS
STRIDE = LEV + ROWS
FIRST = 2
H = 3
EDGE_X = (0, 1, 2, 13, 14, 15)
INNER_X = tuple(range(3, 13))


def roll(value, shift):
    return pltpu.roll(value, shift % LANES, 1)


def split(value):
    high = value.astype(jnp.bfloat16)
    return high, (value - high.astype(jnp.float32)).astype(jnp.bfloat16)


def fill_stencil(stencil):
    row = lax.broadcasted_iota(jnp.int32, (LANES, LANES), 0)
    column = lax.broadcasted_iota(jnp.int32, (LANES, LANES), 1)
    for block in range(4):
        offset = row - column + (2 if block < 2 else 3)
        weights = (1.0, -8.0, 37.0, 37.0, -8.0, 1.0) if block % 2 == 0 else (-1.0, 5.0, -10.0, 10.0, -5.0, 1.0)
        band = jnp.zeros((LANES, LANES), jnp.float32)
        for at, weight in enumerate(weights):
            band = jnp.where(offset == at, weight, band)
        band = band.astype(jnp.bfloat16)
        for part in range(2):
            stencil[pl.ds(part * LANES, LANES), pl.ds(block * LANES, LANES)] = band


def urban(counts, cols, classes, table, wall, indoor, out, wall_out, indoor_out, body, heat_pad):
    slots = cols.shape[1]
    column = cols[...]
    col_x = column // LANES
    col_y = column % LANES
    live = lax.broadcasted_iota(jnp.int32, (1, slots), 1) < counts[0]
    onehot = (lax.broadcasted_iota(jnp.int32, (LANES, slots), 0) == col_y).astype(jnp.float32)
    ncls = table.shape[0]
    picked = (lax.broadcasted_iota(jnp.int32, (ncls, slots), 0) == classes[...]).astype(jnp.float32)
    areas = lax.dot_general(
        table[...], picked, (((0,), (0,)), ((), ())), precision=lax.Precision.HIGHEST, preferred_element_type=jnp.float32
    )
    lowest = out[:, 0, pl.ds(0, LOW), :]
    gathered = jnp.dot(
        lowest.reshape(CX * LOW, LANES), onehot, precision=lax.Precision.HIGHEST, preferred_element_type=jnp.float32
    ).reshape(CX, LOW, slots)
    air = jnp.zeros((LOW, slots), jnp.float32)
    for x in range(CX):
        air = jnp.where(col_x == x, gathered[x], air)
    walls = wall[...]
    room = indoor[...]
    top = walls[0:1]
    heat = heat_coef * areas * (top - air[:UL])
    first = top - wall_coef * jnp.sum(heat, axis=0, keepdims=True) + conduct * (walls[1:2] - top)
    middle = walls[1:-1] + conduct * (walls[:-2] - 2.0 * walls[1:-1] + walls[2:])
    bottom = walls[NWL - 1 : NWL]
    last = bottom + conduct * (walls[NWL - 2 : NWL - 1] - bottom) + inner_coef * (room - bottom)
    wall_out[0:1] = jnp.where(live, first, top)
    wall_out[1 : NWL - 1] = jnp.where(live, middle, walls[1:-1])
    wall_out[NWL - 1 : NWL] = jnp.where(live, last, bottom)
    indoor_out[...] = jnp.where(live, room + room_coef * (bottom - room), room)
    heat_pad[...] = jnp.zeros_like(heat_pad)
    heat_pad[0:UL] = jnp.where(live, flux_coef * heat, 0.0)
    padded = heat_pad[...]
    for x in range(CX):
        body[x] = jnp.where(col_x == x, padded, 0.0)
    spread = lax.dot_general(
        body[...].reshape(CX * LOW, slots), onehot, (((1,), (1,)), ((), ())),
        precision=lax.Precision.HIGHEST, preferred_element_type=jnp.float32,
    )
    out[:, 0, pl.ds(0, LOW), :] = out[:, 0, pl.ds(0, LOW), :] + spread.reshape(CX, LOW, LANES)


def step_kernel(
    scal, wind, mapf, counts, cols, classes, table, wall, indoor, out, wall_out, indoor_out,
    field0, field1, field2, windx, windy, facex, face_r, face_l, edge_weight, square, give_n, give_s, got_s, got_n,
    wpack, wgot, mapbuf, stencil, cells, across,
    load_s, load_w, load_m, sx, rx, sy, ry, swx, rwx, swy, rwy,
    cols_buf, classes_buf, table_buf, wall_buf, indoor_buf, spread_in, heat_pad, load_u,
):
    fields = (field0, field1, field2)
    gx, gy = lax.axis_index("gx"), lax.axis_index("gy")
    nx, ny = lax.axis_size("gx"), lax.axis_size("gy")
    east, west = {"gx": lax.rem(gx + 1, nx)}, {"gx": lax.rem(gx + nx - 1, nx)}
    north, south = {"gy": lax.rem(gy + 1, ny)}, {"gy": lax.rem(gy + ny - 1, ny)}

    barrier = pltpu.get_barrier_semaphore()
    for device in (east, west, north, south):
        pl.semaphore_signal(barrier, inc=1, device_id=device, device_id_type=MESH)

    def load_scalar(x):
        return pltpu.make_async_copy(scal.at[:, :, x, :], field0.at[H + x, :, pl.ds(0, LEV), :], load_s.at[x])

    def load_wind(which, x):
        target = (windx.at[1 + x] if which == 0 else windy.at[x]).at[pl.ds(0, LEV), :]
        return pltpu.make_async_copy(wind.at[which, :, x, :], target, load_w.at[which, x])

    load_map = pltpu.make_async_copy(mapf, mapbuf, load_m)
    for x in EDGE_X:
        load_scalar(x).start()
    load_wind(0, 0).start()
    load_wind(0, CX - 1).start()
    for x in range(CX):
        load_wind(1, x).start()
    for x in INNER_X:
        load_scalar(x).start()
    for x in range(1, CX - 1):
        load_wind(0, x).start()
    load_map.start()
    urban_loads = [
        pltpu.make_async_copy(source, target, load_u.at[n])
        for n, (source, target) in enumerate(
            ((cols, cols_buf), (classes, classes_buf), (table, table_buf), (wall, wall_buf), (indoor, indoor_buf))
        )
    ]
    for copy in urban_loads:
        copy.start()

    def remote(src, dst, send, recv, device):
        return pltpu.make_async_remote_copy(
            src_ref=src, dst_ref=dst, send_sem=send, recv_sem=recv, device_id=device, device_id_type=MESH
        )

    def rows_of(k):
        return pl.ds(pl.multiple_of(k * ROWS, ROWS), ROWS)

    def x_copies(sec, k):
        rows = rows_of(k)
        return (
            remote(fields[sec].at[pl.ds(CX, H), :, rows, :], fields[sec].at[pl.ds(0, H), :, rows, :],
                   sx.at[sec, k, 0], rx.at[sec, k, 0], east),
            remote(fields[sec].at[pl.ds(H, H), :, rows, :], fields[sec].at[pl.ds(CX + H, H), :, rows, :],
                   sx.at[sec, k, 1], rx.at[sec, k, 1], west),
        )

    def y_copies(sec, k):
        return (
            remote(give_n.at[sec, k], got_s.at[sec, k], sy.at[sec, k, 0], ry.at[sec, k, 0], north),
            remote(give_s.at[sec, k], got_n.at[sec, k], sy.at[sec, k, 1], ry.at[sec, k, 1], south),
        )

    wx_copies = (
        remote(windx.at[CX, pl.ds(0, LEV), :], windx.at[0, pl.ds(0, LEV), :], swx.at[0], rwx.at[0], east),
        remote(windx.at[1, pl.ds(0, LEV), :], windx.at[CX + 1, pl.ds(0, LEV), :], swx.at[1], rwx.at[1], west),
    )
    wy_copies = (
        remote(wpack.at[0], wgot.at[0], swy.at[0], rwy.at[0], north),
        remote(wpack.at[1], wgot.at[1], swy.at[1], rwy.at[1], south),
    )

    for x in EDGE_X:
        load_scalar(x).wait()
    load_wind(0, 0).wait()
    load_wind(0, CX - 1).wait()
    pl.semaphore_wait(barrier, 4)
    for copy in wx_copies:
        copy.start()

    def send_first(k, carry):
        for copy in x_copies(0, k):
            copy.start()
        return carry

    lax.fori_loop(0, FIRST, send_first, 0)

    lane = lax.broadcasted_iota(jnp.int32, (ROWS, LANES), 1)
    slot = lane // 8
    inside = lane % 8
    low = inside < 3

    def pack_send(sec, k, pair, first, second):
        give_n[sec, k, pair] = jnp.where(low, first, roll(second, 3))
        give_s[sec, k, pair] = jnp.where(low, roll(first, -3), second)

    for x in range(CX):
        load_wind(1, x).wait()
    to_n = jnp.zeros((ROWS, LANES), jnp.float32)
    to_s = jnp.zeros((ROWS, LANES), jnp.float32)
    lanes = lax.broadcasted_iota(jnp.int32, (LEV, LANES), 1) // 8
    packed = jnp.zeros((LEV, LANES), jnp.float32)
    for x in range(CX):
        packed = jnp.where(lanes == x, roll(windy[x, pl.ds(0, LEV), :], 8 * x + 3), packed)
    for k in range(CHUNKS):
        piece = packed[k * ROWS : (k + 1) * ROWS]
        to_n = jnp.where(inside == k, roll(piece, k - 2), to_n)
        to_s = jnp.where(inside == k, roll(piece, k - 3), to_s)
    wpack[0] = to_n
    wpack[1] = to_s
    for copy in wy_copies:
        copy.start()

    for x in INNER_X:
        load_scalar(x).wait()

    many = lax.broadcasted_iota(jnp.int32, (NSC * ROWS, LANES), 1) // 8

    def pack_first(k, carry):
        rows = rows_of(k)
        packed = jnp.zeros((NSC * ROWS, LANES), jnp.float32)
        for x in range(CX):
            value = field0[H + x, :, rows, :].reshape(NSC * ROWS, LANES)
            packed = jnp.where(many == x, roll(value, 8 * x + 3), packed)
        for pair in range(2):
            at = 2 * pair * ROWS
            pack_send(0, k, pair, packed[at : at + ROWS], packed[at + ROWS : at + 2 * ROWS])
        for copy in y_copies(0, k):
            copy.start()

        @pl.when(k >= FIRST)
        def _():
            send_first(k, carry)

        return carry

    lax.fori_loop(0, CHUNKS, pack_first, 0)
    fill_stencil(stencil)

    load_map.wait()
    for x in range(CX):
        factor = jnp.broadcast_to(mapbuf[pl.ds(x, 1), :], (ROWS, LANES))
        minus = factor * factor
        square[0, x] = minus * (1.0 / 3.0)
        square[1, x] = minus * 0.5
        square[2, x] = minus
    for x in range(1, CX - 1):
        load_wind(0, x).wait()
    for copy in wx_copies:
        copy.wait_recv()
    for copy in wy_copies:
        copy.wait_recv()

    from_s = wgot[0]
    from_n = wgot[1]
    half_levels = LEV // 2
    lanes = lax.broadcasted_iota(jnp.int32, (half_levels, LANES), 1)
    slots, within = lanes // 8, lanes % 8
    below = within < 3
    for part in range(2):
        rows = pl.ds(part * half_levels, half_levels)
        for x in range(CX + 1):
            facex[x, rows, :] = (windx[x, rows, :] + windx[x + 1, rows, :]) * (1.0 / 120.0)
        merged = jnp.concatenate(
            [
                jnp.where(low, roll(from_s, 2 - k), roll(from_n, 3 - k))
                for k in range(part * CHUNKS // 2, (part + 1) * CHUNKS // 2)
            ],
            axis=0,
        )
        zero = jnp.zeros((half_levels, LANES), jnp.float32)

        def faces(x, packed):
            left, right = packed
            centre = windy[x, rows, :]
            halo = roll(merged, -(8 * x + 3))
            behind = (roll(jnp.where(lanes == LANES - 1, halo, centre), 1) + centre) * (1.0 / 120.0)
            ahead = (roll(jnp.where(lanes == 0, halo, centre), -1) + centre) * (1.0 / 120.0)
            face_l[x, rows, :] = behind
            face_r[x, rows, :] = ahead
            return (
                jnp.where(slots == x, roll(behind, 8 * x + 3), left),
                jnp.where(slots == x, roll(ahead, 8 * x + 3), right),
            )

        left, right = zero, zero
        for x in range(CX):
            left, right = faces(x, (left, right))
        right_abs, left_abs = jnp.abs(right), jnp.abs(left)
        three = jnp.where(below, right - right_abs, jnp.where(within < 6, -(left + left_abs), zero))
        two = jnp.where(
            (within == 1) | (within == 2),
            (5.0 * right_abs - 8.0 * right) + (left_abs - left),
            jnp.where((within == 3) | (within == 4), (right + right_abs) + (8.0 * left + 5.0 * left_abs), zero),
        )
        one = jnp.where(
            within == 2,
            (37.0 * right - 10.0 * right_abs) + (8.0 * left - 5.0 * left_abs),
            jnp.where(within == 3, -(8.0 * right + 5.0 * right_abs) - (37.0 * left + 10.0 * left_abs), zero),
        )
        edge_weight[0, rows, :] = one
        edge_weight[1, rows, :] = two
        edge_weight[2, rows, :] = three

    size = NSC * ROWS
    half = CX // 2
    edge = (lane < H) | (lane >= LANES - H)

    def section(sec, k, last):
        rows = rows_of(k)
        for part in range(2):
            for x in range(part * half, (part + 1) * half):
                at = pl.ds(x * size, size)
                high, rest = split(fields[sec][H + x, :, rows, :].reshape(size, LANES))
                cells[at, 0:LANES] = high
                cells[at, LANES : 2 * LANES] = rest
            at = pl.ds(part * half * size, half * size)
            across[at, :] = jnp.dot(cells[at, :], stencil[...], preferred_element_type=jnp.float32)
        for pair in range(2):
            from_south, from_north = got_s[sec, k, pair], got_n[sec, k, pair]
            halos = (
                jnp.where(low, from_south, roll(from_north, 3)),
                jnp.where(low, roll(from_south, -3), from_north),
            )
            added = []
            for halo in halos:
                added.append(
                    sum(
                        edge_weight[r - 1, rows, :] * jnp.where(low, roll(halo, -r), roll(halo, r))
                        for r in (1, 2, 3)
                    )
                )
            members = (2 * pair, 2 * pair + 1)
            packs = {s: jnp.zeros((ROWS, LANES), jnp.float32) for s in members}
            q, g, d2, d3, d4, even, flux = ({s: {} for s in members} for _ in range(7))
            for i in range(CX + 2 * H):
                f, x = i - 5, i - 6
                if f >= 0:
                    speed = facex[f, rows, :]
                    speed_abs = jnp.abs(speed)
                if x >= 0:
                    ahead, behind, scale = face_r[x, rows, :], face_l[x, rows, :], square[sec, x]
                    ahead_abs, behind_abs = jnp.abs(ahead), jnp.abs(behind)
                for s in members:
                    q[s][i] = fields[sec][i, s, rows, :]
                    if i >= 1:
                        g[s][i - 1] = q[s][i] - q[s][i - 1]
                    if i >= 2:
                        d2[s][i - 1] = g[s][i - 1] - g[s][i - 2]
                    if i >= 3:
                        d3[s][i - 2] = d2[s][i - 1] - d2[s][i - 2]
                    if i >= 4:
                        d4[s][i - 2] = d3[s][i - 2] - d3[s][i - 3]
                        even[s][i - 2] = (d4[s][i - 2] - 5.0 * d2[s][i - 2]) + 30.0 * q[s][i - 2]
                    if f >= 0:
                        flux[s][f] = speed * (even[s][i - 3] + even[s][i - 2]) - speed_abs * (d4[s][i - 2] - d4[s][i - 3])
                    if x >= 0:
                        at = pl.ds(x * size + s * ROWS, ROWS)
                        total = flux[s][x + 1] - flux[s][x]
                        total += ahead * across[at, 0:LANES] - ahead_abs * across[at, LANES : 2 * LANES]
                        total -= behind * across[at, 2 * LANES : 3 * LANES] - behind_abs * across[at, 3 * LANES : 4 * LANES]
                        total += jnp.where(edge, roll(added[s % 2], -(8 * x + 3)), 0.0)
                        new = (field0[H + x, s, rows, :] if sec else q[s][H + x]) - scale * total
                        if last:
                            out[x, s, rows, :] = new
                        else:
                            fields[sec + 1][H + x, s, rows, :] = new
                            packs[s] = jnp.where(slot == x, roll(new, 8 * x + 3), packs[s])
            if not last:
                pack_send(sec + 1, k, pair, packs[members[0]], packs[members[1]])

    for sec in range(2):

        def early(k, carry, sec=sec):
            for copy in x_copies(sec, k) + y_copies(sec, k):
                copy.wait_recv()
            section(sec, k, False)
            for copy in y_copies(sec + 1, k) + x_copies(sec + 1, k):
                copy.start()
            return carry

        lax.fori_loop(0, CHUNKS, early, 0)

    def late(k, carry):
        for copy in x_copies(2, k) + y_copies(2, k):
            copy.wait_recv()
        section(2, k, True)

        @pl.when(k == LOW // ROWS - 1)
        def _():
            for copy in urban_loads:
                copy.wait()
            urban(counts, cols_buf, classes_buf, table_buf, wall_buf, indoor_buf, out, wall_out, indoor_out, spread_in, heat_pad)

        return carry

    lax.fori_loop(0, CHUNKS, late, 0)

    for copy in wx_copies + wy_copies:
        copy.wait_send()

    def finish(k, carry):
        for sec in range(3):
            for copy in x_copies(sec, k) + y_copies(sec, k):
                copy.wait_send()
        return carry

    lax.fori_loop(0, CHUNKS, finish, 0)


def advance(scalars, winds, map_factor, counts, cols, classes, table, wall, indoor):
    f32, i32 = jnp.float32, jnp.int32
    dma = pltpu.SemaphoreType.DMA
    slots = wall.shape[1]
    vmem = pl.BlockSpec(memory_space=pltpu.VMEM)
    anywhere = pl.BlockSpec(memory_space=pl.ANY)
    grids = (scalars, winds, map_factor)
    columns = (cols.reshape(1, slots), classes.reshape(1, slots), table, wall, indoor.reshape(1, slots))
    operands = [pltpu.with_memory_space_constraint(array, pltpu.HBM) for array in grids + columns]
    operands.insert(len(grids), counts)
    return pl.pallas_call(
        step_kernel,
        out_shape=(
            jax.ShapeDtypeStruct((CX, NSC, LEV, LANES), f32),
            jax.ShapeDtypeStruct((NWL, slots), f32),
            jax.ShapeDtypeStruct((1, slots), f32),
        ),
        in_specs=[anywhere] * 3 + [pl.BlockSpec(memory_space=pltpu.SMEM)] + [anywhere] * 5,
        out_specs=(vmem, vmem, vmem),
        scratch_shapes=[
            pltpu.VMEM((CX + 2 * H, NSC, STRIDE, LANES), f32),
            pltpu.VMEM((CX + 2 * H, NSC, STRIDE, LANES), f32),
            pltpu.VMEM((CX + 2 * H, NSC, STRIDE, LANES), f32),
            pltpu.VMEM((CX + 2, STRIDE, LANES), f32),
            pltpu.VMEM((CX, STRIDE, LANES), f32),
            pltpu.VMEM((CX + 1, STRIDE, LANES), f32),
            pltpu.VMEM((CX, STRIDE, LANES), f32),
            pltpu.VMEM((CX, STRIDE, LANES), f32),
            pltpu.VMEM((H, LEV, LANES), f32),
            pltpu.VMEM((3, CX, ROWS, LANES), f32),
            pltpu.VMEM((3, CHUNKS, 2, ROWS, LANES), f32),
            pltpu.VMEM((3, CHUNKS, 2, ROWS, LANES), f32),
            pltpu.VMEM((3, CHUNKS, 2, ROWS, LANES), f32),
            pltpu.VMEM((3, CHUNKS, 2, ROWS, LANES), f32),
            pltpu.VMEM((2, ROWS, LANES), f32),
            pltpu.VMEM((2, ROWS, LANES), f32),
            pltpu.VMEM((CX, LANES), f32),
            pltpu.VMEM((2 * LANES, 4 * LANES), jnp.bfloat16),
            pltpu.VMEM((CX * NSC * ROWS, 2 * LANES), jnp.bfloat16),
            pltpu.VMEM((CX * NSC * ROWS, 4 * LANES), f32),
            dma((CX,)),
            dma((2, CX)),
            dma(()),
            dma((3, CHUNKS, 2)),
            dma((3, CHUNKS, 2)),
            dma((3, CHUNKS, 2)),
            dma((3, CHUNKS, 2)),
            dma((2,)),
            dma((2,)),
            dma((2,)),
            dma((2,)),
            pltpu.VMEM((1, slots), i32),
            pltpu.VMEM((1, slots), i32),
            pltpu.VMEM(table.shape, f32),
            pltpu.VMEM((NWL, slots), f32),
            pltpu.VMEM((1, slots), f32),
            pltpu.VMEM((CX, LOW, slots), f32),
            pltpu.VMEM((LOW, slots), f32),
            dma((5,)),
        ],
        compiler_params=pltpu.CompilerParams(collective_id=0, has_side_effects=True, vmem_limit_bytes=32 << 20),
        name="advance",
    )(*operands)


def store_kernel(adv, wall, indoor, out, wall_out, indoor_out, sem, sem_wall, sem_indoor):
    copies = [
        pltpu.make_async_copy(adv.at[x], out.at[:, :, x, :], sem.at[x]) for x in range(CX)
    ]
    copies.append(pltpu.make_async_copy(wall, wall_out, sem_wall))
    copies.append(pltpu.make_async_copy(indoor, indoor_out, sem_indoor))
    for copy in copies:
        copy.start()
    for copy in copies:
        copy.wait()


def store(adv, wall, indoor):
    f32 = jnp.float32
    anywhere = pl.BlockSpec(memory_space=pl.ANY)
    dma = pltpu.SemaphoreType.DMA
    return pl.pallas_call(
        store_kernel,
        out_shape=(
            jax.ShapeDtypeStruct((NSC, LEV, CX, LANES), f32),
            jax.ShapeDtypeStruct(wall.shape, f32),
            jax.ShapeDtypeStruct(indoor.shape, f32),
        ),
        in_specs=[anywhere] * 3,
        out_specs=(anywhere,) * 3,
        scratch_shapes=[dma((CX,)), dma(()), dma(())],
        compiler_params=pltpu.CompilerParams(vmem_limit_bytes=4 << 20),
        name="store",
    )(adv, wall, indoor)


def per_device(scalars, winds, map_factor, urban_counts, urban_cols, street_class, area_table, wall_temp, indoor_temp):
    adv, walls, rooms = advance(
        scalars, winds, map_factor, urban_counts, urban_cols, street_class, area_table, wall_temp, indoor_temp
    )
    scalars_out, wall_out, indoor_out = store(adv, walls, rooms)
    return (scalars_out, wall_out, indoor_out.reshape(indoor_temp.shape))


def solution(mesh):
    in_specs = (
        P(None, None, "gx", "gy"),
        P(None, None, "gx", "gy"),
        P("gx", "gy"),
        P(("gx", "gy")),
        P(("gx", "gy")),
        P(("gx", "gy")),
        P(),
        P(None, ("gx", "gy")),
        P(("gx", "gy")),
    )
    out_specs = (P(None, None, "gx", "gy"), P(None, ("gx", "gy")), P(("gx", "gy")))
    return jax.shard_map(per_device, mesh=mesh, in_specs=in_specs, out_specs=out_specs, check_vma=False)
```

```python
import jax
import jax.numpy as jnp
from jax import lax
from jax.experimental import pallas as pl
from jax.experimental.pallas import tpu as pltpu
from jax.sharding import PartitionSpec as P

MESH = pl.DeviceIdType.MESH
UL = 10
NWL = 10
LOW = 16

heat_coef = 0.5
wall_coef = 0.05
conduct = 0.3
inner_coef = 0.2
room_coef = 0.1
flux_coef = 0.5

CX = 16
LANES = 128
NSC = 4
LEV = 64
ROWS = 8
CHUNKS = LEV // ROWS
STRIDE = LEV + ROWS
FIRST = 2
H = 3
EDGE_X = (0, 1, 2, 13, 14, 15)
INNER_X = tuple(range(3, 13))


def roll(value, shift):
    return pltpu.roll(value, shift % LANES, 1)


def split(value):
    high = value.astype(jnp.bfloat16)
    return high, (value - high.astype(jnp.float32)).astype(jnp.bfloat16)


def fill_stencil(stencil):
    row = lax.broadcasted_iota(jnp.int32, (LANES, LANES), 0)
    column = lax.broadcasted_iota(jnp.int32, (LANES, LANES), 1)
    for block in range(4):
        offset = row - column + (2 if block < 2 else 3)
        weights = (1.0, -8.0, 37.0, 37.0, -8.0, 1.0) if block % 2 == 0 else (-1.0, 5.0, -10.0, 10.0, -5.0, 1.0)
        band = jnp.zeros((LANES, LANES), jnp.float32)
        for at, weight in enumerate(weights):
            band = jnp.where(offset == at, weight, band)
        band = band.astype(jnp.bfloat16)
        for part in range(2):
            stencil[pl.ds(part * LANES, LANES), pl.ds(block * LANES, LANES)] = band


def urban(counts, cols, classes, table, wall, indoor, out, wall_out, indoor_out, body, heat_pad):
    slots = cols.shape[1]
    column = cols[...]
    col_x = column // LANES
    col_y = column % LANES
    live = lax.broadcasted_iota(jnp.int32, (1, slots), 1) < counts[0]
    onehot = (lax.broadcasted_iota(jnp.int32, (LANES, slots), 0) == col_y).astype(jnp.float32)
    ncls = table.shape[0]
    picked = (lax.broadcasted_iota(jnp.int32, (ncls, slots), 0) == classes[...]).astype(jnp.float32)
    areas = lax.dot_general(
        table[...], picked, (((0,), (0,)), ((), ())), precision=lax.Precision.HIGHEST, preferred_element_type=jnp.float32
    )
    lowest = out[:, 0, pl.ds(0, LOW), :]
    gathered = jnp.dot(
        lowest.reshape(CX * LOW, LANES), onehot, precision=lax.Precision.HIGHEST, preferred_element_type=jnp.float32
    ).reshape(CX, LOW, slots)
    air = jnp.zeros((LOW, slots), jnp.float32)
    for x in range(CX):
        air = jnp.where(col_x == x, gathered[x], air)
    walls = wall[...]
    room = indoor[...]
    top = walls[0:1]
    heat = heat_coef * areas * (top - air[:UL])
    first = top - wall_coef * jnp.sum(heat, axis=0, keepdims=True) + conduct * (walls[1:2] - top)
    middle = walls[1:-1] + conduct * (walls[:-2] - 2.0 * walls[1:-1] + walls[2:])
    bottom = walls[NWL - 1 : NWL]
    last = bottom + conduct * (walls[NWL - 2 : NWL - 1] - bottom) + inner_coef * (room - bottom)
    wall_out[0:1] = jnp.where(live, first, top)
    wall_out[1 : NWL - 1] = jnp.where(live, middle, walls[1:-1])
    wall_out[NWL - 1 : NWL] = jnp.where(live, last, bottom)
    indoor_out[...] = jnp.where(live, room + room_coef * (bottom - room), room)
    heat_pad[...] = jnp.zeros_like(heat_pad)
    heat_pad[0:UL] = jnp.where(live, flux_coef * heat, 0.0)
    padded = heat_pad[...]
    for x in range(CX):
        body[x] = jnp.where(col_x == x, padded, 0.0)
    spread = lax.dot_general(
        body[...].reshape(CX * LOW, slots), onehot, (((1,), (1,)), ((), ())),
        precision=lax.Precision.HIGHEST, preferred_element_type=jnp.float32,
    )
    out[:, 0, pl.ds(0, LOW), :] = out[:, 0, pl.ds(0, LOW), :] + spread.reshape(CX, LOW, LANES)


def step_kernel(
    scal, wind, mapf, counts, cols, classes, table, wall, indoor, out, wall_out, indoor_out,
    field0, field1, field2, windx, windy, facex, face_r, face_l, edge_weight, square, give_n, give_s, got_s, got_n,
    wpack, wgot, mapbuf, stencil, cells, across,
    load_s, load_w, load_m, sx, rx, sy, ry, swx, rwx, swy, rwy,
    cols_buf, classes_buf, table_buf, wall_buf, indoor_buf, spread_in, heat_pad, load_u,
):
    fields = (field0, field1, field2)
    gx, gy = lax.axis_index("gx"), lax.axis_index("gy")
    nx, ny = lax.axis_size("gx"), lax.axis_size("gy")
    east, west = {"gx": lax.rem(gx + 1, nx)}, {"gx": lax.rem(gx + nx - 1, nx)}
    north, south = {"gy": lax.rem(gy + 1, ny)}, {"gy": lax.rem(gy + ny - 1, ny)}

    barrier = pltpu.get_barrier_semaphore()
    for device in (east, west, north, south):
        pl.semaphore_signal(barrier, inc=1, device_id=device, device_id_type=MESH)

    def load_scalar(x):
        return pltpu.make_async_copy(scal.at[:, :, x, :], field0.at[H + x, :, pl.ds(0, LEV), :], load_s.at[x])

    def load_wind(which, x):
        target = (windx.at[1 + x] if which == 0 else windy.at[x]).at[pl.ds(0, LEV), :]
        return pltpu.make_async_copy(wind.at[which, :, x, :], target, load_w.at[which, x])

    load_map = pltpu.make_async_copy(mapf, mapbuf, load_m)
    for x in EDGE_X:
        load_scalar(x).start()
    load_wind(0, 0).start()
    load_wind(0, CX - 1).start()
    for x in range(CX):
        load_wind(1, x).start()
    for x in INNER_X:
        load_scalar(x).start()
    for x in range(1, CX - 1):
        load_wind(0, x).start()
    load_map.start()
    urban_loads = [
        pltpu.make_async_copy(source, target, load_u.at[n])
        for n, (source, target) in enumerate(
            ((cols, cols_buf), (classes, classes_buf), (table, table_buf), (wall, wall_buf), (indoor, indoor_buf))
        )
    ]
    for copy in urban_loads:
        copy.start()

    def remote(src, dst, send, recv, device):
        return pltpu.make_async_remote_copy(
            src_ref=src, dst_ref=dst, send_sem=send, recv_sem=recv, device_id=device, device_id_type=MESH
        )

    def rows_of(k):
        return pl.ds(pl.multiple_of(k * ROWS, ROWS), ROWS)

    def x_copies(sec, k):
        rows = rows_of(k)
        return (
            remote(fields[sec].at[pl.ds(CX, H), :, rows, :], fields[sec].at[pl.ds(0, H), :, rows, :],
                   sx.at[sec, k, 0], rx.at[sec, k, 0], east),
            remote(fields[sec].at[pl.ds(H, H), :, rows, :], fields[sec].at[pl.ds(CX + H, H), :, rows, :],
                   sx.at[sec, k, 1], rx.at[sec, k, 1], west),
        )

    def y_copies(sec, k):
        return (
            remote(give_n.at[sec, k], got_s.at[sec, k], sy.at[sec, k, 0], ry.at[sec, k, 0], north),
            remote(give_s.at[sec, k], got_n.at[sec, k], sy.at[sec, k, 1], ry.at[sec, k, 1], south),
        )

    wx_copies = (
        remote(windx.at[CX, pl.ds(0, LEV), :], windx.at[0, pl.ds(0, LEV), :], swx.at[0], rwx.at[0], east),
        remote(windx.at[1, pl.ds(0, LEV), :], windx.at[CX + 1, pl.ds(0, LEV), :], swx.at[1], rwx.at[1], west),
    )
    wy_copies = (
        remote(wpack.at[0], wgot.at[0], swy.at[0], rwy.at[0], north),
        remote(wpack.at[1], wgot.at[1], swy.at[1], rwy.at[1], south),
    )

    for x in EDGE_X:
        load_scalar(x).wait()
    load_wind(0, 0).wait()
    load_wind(0, CX - 1).wait()
    pl.semaphore_wait(barrier, 4)
    for copy in wx_copies:
        copy.start()

    def send_first(k, carry):
        for copy in x_copies(0, k):
            copy.start()
        return carry

    lax.fori_loop(0, FIRST, send_first, 0)

    lane = lax.broadcasted_iota(jnp.int32, (ROWS, LANES), 1)
    slot = lane // 8
    inside = lane % 8
    low = inside < 3

    def pack_send(sec, k, pair, first, second):
        give_n[sec, k, pair] = jnp.where(low, first, roll(second, 3))
        give_s[sec, k, pair] = jnp.where(low, roll(first, -3), second)

    for x in range(CX):
        load_wind(1, x).wait()
    to_n = jnp.zeros((ROWS, LANES), jnp.float32)
    to_s = jnp.zeros((ROWS, LANES), jnp.float32)
    lanes = lax.broadcasted_iota(jnp.int32, (LEV, LANES), 1) // 8
    packed = jnp.zeros((LEV, LANES), jnp.float32)
    for x in range(CX):
        packed = jnp.where(lanes == x, roll(windy[x, pl.ds(0, LEV), :], 8 * x + 3), packed)
    for k in range(CHUNKS):
        piece = packed[k * ROWS : (k + 1) * ROWS]
        to_n = jnp.where(inside == k, roll(piece, k - 2), to_n)
        to_s = jnp.where(inside == k, roll(piece, k - 3), to_s)
    wpack[0] = to_n
    wpack[1] = to_s
    for copy in wy_copies:
        copy.start()

    for x in INNER_X:
        load_scalar(x).wait()

    many = lax.broadcasted_iota(jnp.int32, (NSC * ROWS, LANES), 1) // 8

    def pack_first(k, carry):
        rows = rows_of(k)
        packed = jnp.zeros((NSC * ROWS, LANES), jnp.float32)
        for x in range(CX):
            value = field0[H + x, :, rows, :].reshape(NSC * ROWS, LANES)
            packed = jnp.where(many == x, roll(value, 8 * x + 3), packed)
        for pair in range(2):
            at = 2 * pair * ROWS
            pack_send(0, k, pair, packed[at : at + ROWS], packed[at + ROWS : at + 2 * ROWS])
        for copy in y_copies(0, k):
            copy.start()

        @pl.when(k >= FIRST)
        def _():
            send_first(k, carry)

        return carry

    lax.fori_loop(0, CHUNKS, pack_first, 0)
    fill_stencil(stencil)

    load_map.wait()
    for x in range(CX):
        factor = jnp.broadcast_to(mapbuf[pl.ds(x, 1), :], (ROWS, LANES))
        minus = factor * factor
        square[0, x] = minus * (1.0 / 3.0)
        square[1, x] = minus * 0.5
        square[2, x] = minus
    for x in range(1, CX - 1):
        load_wind(0, x).wait()
    for copy in wx_copies:
        copy.wait_recv()
    for copy in wy_copies:
        copy.wait_recv()

    from_s = wgot[0]
    from_n = wgot[1]
    half_levels = LEV // 2
    lanes = lax.broadcasted_iota(jnp.int32, (half_levels, LANES), 1)
    slots, within = lanes // 8, lanes % 8
    below = within < 3

    def prepare(part):
        rows = pl.ds(part * half_levels, half_levels)
        for x in range(CX + 1):
            facex[x, rows, :] = (windx[x, rows, :] + windx[x + 1, rows, :]) * (1.0 / 120.0)
        merged = jnp.concatenate(
            [
                jnp.where(low, roll(from_s, 2 - k), roll(from_n, 3 - k))
                for k in range(part * CHUNKS // 2, (part + 1) * CHUNKS // 2)
            ],
            axis=0,
        )
        zero = jnp.zeros((half_levels, LANES), jnp.float32)

        def faces(x, packed):
            left, right = packed
            centre = windy[x, rows, :]
            halo = roll(merged, -(8 * x + 3))
            behind = (roll(jnp.where(lanes == LANES - 1, halo, centre), 1) + centre) * (1.0 / 120.0)
            ahead = (roll(jnp.where(lanes == 0, halo, centre), -1) + centre) * (1.0 / 120.0)
            face_l[x, rows, :] = behind
            face_r[x, rows, :] = ahead
            return (
                jnp.where(slots == x, roll(behind, 8 * x + 3), left),
                jnp.where(slots == x, roll(ahead, 8 * x + 3), right),
            )

        left, right = zero, zero
        for x in range(CX):
            left, right = faces(x, (left, right))
        right_abs, left_abs = jnp.abs(right), jnp.abs(left)
        three = jnp.where(below, right - right_abs, jnp.where(within < 6, -(left + left_abs), zero))
        two = jnp.where(
            (within == 1) | (within == 2),
            (5.0 * right_abs - 8.0 * right) + (left_abs - left),
            jnp.where((within == 3) | (within == 4), (right + right_abs) + (8.0 * left + 5.0 * left_abs), zero),
        )
        one = jnp.where(
            within == 2,
            (37.0 * right - 10.0 * right_abs) + (8.0 * left - 5.0 * left_abs),
            jnp.where(within == 3, -(8.0 * right + 5.0 * right_abs) - (37.0 * left + 10.0 * left_abs), zero),
        )
        edge_weight[0, rows, :] = one
        edge_weight[1, rows, :] = two
        edge_weight[2, rows, :] = three

    prepare(0)
    size = NSC * ROWS
    half = CX // 2
    edge = (lane < H) | (lane >= LANES - H)

    def section(sec, k, last):
        rows = rows_of(k)
        for part in range(2):
            for x in range(part * half, (part + 1) * half):
                at = pl.ds(x * size, size)
                high, rest = split(fields[sec][H + x, :, rows, :].reshape(size, LANES))
                cells[at, 0:LANES] = high
                cells[at, LANES : 2 * LANES] = rest
            at = pl.ds(part * half * size, half * size)
            across[at, :] = jnp.dot(cells[at, :], stencil[...], preferred_element_type=jnp.float32)
        for pair in range(2):
            from_south, from_north = got_s[sec, k, pair], got_n[sec, k, pair]
            halos = (
                jnp.where(low, from_south, roll(from_north, 3)),
                jnp.where(low, roll(from_south, -3), from_north),
            )
            added = []
            for halo in halos:
                added.append(
                    sum(
                        edge_weight[r - 1, rows, :] * jnp.where(low, roll(halo, -r), roll(halo, r))
                        for r in (1, 2, 3)
                    )
                )
            members = (2 * pair, 2 * pair + 1)
            packs = {s: jnp.zeros((ROWS, LANES), jnp.float32) for s in members}
            q, g, d2, d3, d4, even, flux = ({s: {} for s in members} for _ in range(7))
            for i in range(CX + 2 * H):
                f, x = i - 5, i - 6
                if f >= 0:
                    speed = facex[f, rows, :]
                    speed_abs = jnp.abs(speed)
                if x >= 0:
                    ahead, behind, scale = face_r[x, rows, :], face_l[x, rows, :], square[sec, x]
                    ahead_abs, behind_abs = jnp.abs(ahead), jnp.abs(behind)
                for s in members:
                    q[s][i] = fields[sec][i, s, rows, :]
                    if i >= 1:
                        g[s][i - 1] = q[s][i] - q[s][i - 1]
                    if i >= 2:
                        d2[s][i - 1] = g[s][i - 1] - g[s][i - 2]
                    if i >= 3:
                        d3[s][i - 2] = d2[s][i - 1] - d2[s][i - 2]
                    if i >= 4:
                        d4[s][i - 2] = d3[s][i - 2] - d3[s][i - 3]
                        even[s][i - 2] = (d4[s][i - 2] - 5.0 * d2[s][i - 2]) + 30.0 * q[s][i - 2]
                    if f >= 0:
                        flux[s][f] = speed * (even[s][i - 3] + even[s][i - 2]) - speed_abs * (d4[s][i - 2] - d4[s][i - 3])
                    if x >= 0:
                        at = pl.ds(x * size + s * ROWS, ROWS)
                        total = flux[s][x + 1] - flux[s][x]
                        total += ahead * across[at, 0:LANES] - ahead_abs * across[at, LANES : 2 * LANES]
                        total -= behind * across[at, 2 * LANES : 3 * LANES] - behind_abs * across[at, 3 * LANES : 4 * LANES]
                        total += jnp.where(edge, roll(added[s % 2], -(8 * x + 3)), 0.0)
                        new = (field0[H + x, s, rows, :] if sec else q[s][H + x]) - scale * total
                        if last:
                            out[x, s, rows, :] = new
                        else:
                            fields[sec + 1][H + x, s, rows, :] = new
                            packs[s] = jnp.where(slot == x, roll(new, 8 * x + 3), packs[s])
            if not last:
                pack_send(sec + 1, k, pair, packs[members[0]], packs[members[1]])

    for sec in range(2):

        def early(k, carry, sec=sec):
            if sec == 0:

                @pl.when(k == CHUNKS // 2)
                def _():
                    prepare(1)

            for copy in x_copies(sec, k) + y_copies(sec, k):
                copy.wait_recv()
            section(sec, k, False)
            for copy in y_copies(sec + 1, k) + x_copies(sec + 1, k):
                copy.start()
            return carry

        lax.fori_loop(0, CHUNKS, early, 0)

    def late(k, carry):
        for sec in range(2):
            for copy in x_copies(sec, k) + y_copies(sec, k):
                copy.wait_send()
        for copy in x_copies(2, k) + y_copies(2, k):
            copy.wait_recv()
        section(2, k, True)

        @pl.when(k == LOW // ROWS - 1)
        def _():
            for copy in urban_loads:
                copy.wait()
            urban(counts, cols_buf, classes_buf, table_buf, wall_buf, indoor_buf, out, wall_out, indoor_out, spread_in, heat_pad)

        return carry

    lax.fori_loop(0, CHUNKS, late, 0)

    for copy in wx_copies + wy_copies:
        copy.wait_send()

    def finish(k, carry):
        for copy in x_copies(2, k) + y_copies(2, k):
            copy.wait_send()
        return carry

    lax.fori_loop(0, CHUNKS, finish, 0)


def advance(scalars, winds, map_factor, counts, cols, classes, table, wall, indoor):
    f32, i32 = jnp.float32, jnp.int32
    dma = pltpu.SemaphoreType.DMA
    slots = wall.shape[1]
    vmem = pl.BlockSpec(memory_space=pltpu.VMEM)
    anywhere = pl.BlockSpec(memory_space=pl.ANY)
    grids = (scalars, winds, map_factor)
    columns = (cols.reshape(1, slots), classes.reshape(1, slots), table, wall, indoor.reshape(1, slots))
    operands = [pltpu.with_memory_space_constraint(array, pltpu.HBM) for array in grids + columns]
    operands.insert(len(grids), counts)
    return pl.pallas_call(
        step_kernel,
        out_shape=(
            jax.ShapeDtypeStruct((CX, NSC, LEV, LANES), f32),
            jax.ShapeDtypeStruct((NWL, slots), f32),
            jax.ShapeDtypeStruct((1, slots), f32),
        ),
        in_specs=[anywhere] * 3 + [pl.BlockSpec(memory_space=pltpu.SMEM)] + [anywhere] * 5,
        out_specs=(vmem, vmem, vmem),
        scratch_shapes=[
            pltpu.VMEM((CX + 2 * H, NSC, STRIDE, LANES), f32),
            pltpu.VMEM((CX + 2 * H, NSC, STRIDE, LANES), f32),
            pltpu.VMEM((CX + 2 * H, NSC, STRIDE, LANES), f32),
            pltpu.VMEM((CX + 2, STRIDE, LANES), f32),
            pltpu.VMEM((CX, STRIDE, LANES), f32),
            pltpu.VMEM((CX + 1, STRIDE, LANES), f32),
            pltpu.VMEM((CX, STRIDE, LANES), f32),
            pltpu.VMEM((CX, STRIDE, LANES), f32),
            pltpu.VMEM((H, LEV, LANES), f32),
            pltpu.VMEM((3, CX, ROWS, LANES), f32),
            pltpu.VMEM((3, CHUNKS, 2, ROWS, LANES), f32),
            pltpu.VMEM((3, CHUNKS, 2, ROWS, LANES), f32),
            pltpu.VMEM((3, CHUNKS, 2, ROWS, LANES), f32),
            pltpu.VMEM((3, CHUNKS, 2, ROWS, LANES), f32),
            pltpu.VMEM((2, ROWS, LANES), f32),
            pltpu.VMEM((2, ROWS, LANES), f32),
            pltpu.VMEM((CX, LANES), f32),
            pltpu.VMEM((2 * LANES, 4 * LANES), jnp.bfloat16),
            pltpu.VMEM((CX * NSC * ROWS, 2 * LANES), jnp.bfloat16),
            pltpu.VMEM((CX * NSC * ROWS, 4 * LANES), f32),
            dma((CX,)),
            dma((2, CX)),
            dma(()),
            dma((3, CHUNKS, 2)),
            dma((3, CHUNKS, 2)),
            dma((3, CHUNKS, 2)),
            dma((3, CHUNKS, 2)),
            dma((2,)),
            dma((2,)),
            dma((2,)),
            dma((2,)),
            pltpu.VMEM((1, slots), i32),
            pltpu.VMEM((1, slots), i32),
            pltpu.VMEM(table.shape, f32),
            pltpu.VMEM((NWL, slots), f32),
            pltpu.VMEM((1, slots), f32),
            pltpu.VMEM((CX, LOW, slots), f32),
            pltpu.VMEM((LOW, slots), f32),
            dma((5,)),
        ],
        compiler_params=pltpu.CompilerParams(collective_id=0, has_side_effects=True, vmem_limit_bytes=32 << 20),
        name="advance",
    )(*operands)


def store_kernel(adv, wall, indoor, out, wall_out, indoor_out, sem, sem_wall, sem_indoor):
    copies = [
        pltpu.make_async_copy(adv.at[x], out.at[:, :, x, :], sem.at[x]) for x in range(CX)
    ]
    copies.append(pltpu.make_async_copy(wall, wall_out, sem_wall))
    copies.append(pltpu.make_async_copy(indoor, indoor_out, sem_indoor))
    for copy in copies:
        copy.start()
    for copy in copies:
        copy.wait()


def store(adv, wall, indoor):
    f32 = jnp.float32
    anywhere = pl.BlockSpec(memory_space=pl.ANY)
    dma = pltpu.SemaphoreType.DMA
    return pl.pallas_call(
        store_kernel,
        out_shape=(
            jax.ShapeDtypeStruct((NSC, LEV, CX, LANES), f32),
            jax.ShapeDtypeStruct(wall.shape, f32),
            jax.ShapeDtypeStruct(indoor.shape, f32),
        ),
        in_specs=[anywhere] * 3,
        out_specs=(anywhere,) * 3,
        scratch_shapes=[dma((CX,)), dma(()), dma(())],
        compiler_params=pltpu.CompilerParams(vmem_limit_bytes=4 << 20),
        name="store",
    )(adv, wall, indoor)


def per_device(scalars, winds, map_factor, urban_counts, urban_cols, street_class, area_table, wall_temp, indoor_temp):
    adv, walls, rooms = advance(
        scalars, winds, map_factor, urban_counts, urban_cols, street_class, area_table, wall_temp, indoor_temp
    )
    scalars_out, wall_out, indoor_out = store(adv, walls, rooms)
    return (scalars_out, wall_out, indoor_out.reshape(indoor_temp.shape))


def solution(mesh):
    in_specs = (
        P(None, None, "gx", "gy"),
        P(None, None, "gx", "gy"),
        P("gx", "gy"),
        P(("gx", "gy")),
        P(("gx", "gy")),
        P(("gx", "gy")),
        P(),
        P(None, ("gx", "gy")),
        P(("gx", "gy")),
    )
    out_specs = (P(None, None, "gx", "gy"), P(None, ("gx", "gy")), P(("gx", "gy")))
    return jax.shard_map(per_device, mesh=mesh, in_specs=in_specs, out_specs=out_specs, check_vma=False)
```
